256 devices in a mesh: side: 2 (over core), grp: 4 (over y), blk: 32 (over x, z).
Axes of the slice: x: 4, y: 4, z: 8, core: 2. Of those that a mesh axis runs over, the one named last changes fastest.
Arguments:
- node_modes: bfloat16 [3, 131072, 256], P(None, ('grp', 'blk'), 'side'), may hold values from -6 to 6
- node_index: int32 [4, 196608], P(None, ('grp', 'blk')), may hold values from 0 to 1023
- interp: float32 [4, 196608], P(None, ('grp', 'blk')), may hold values from 0.1 to 1
- normals: float32 [3, 196608], P(None, ('grp', 'blk')), may hold values from -6 to 6
- counts: int32 [128, 128], P(None, ('grp', 'blk')), may hold values from 0 to 12, as said below
- inverse_diag: bfloat16 [131072, 1024], P(('grp', 'blk'))
- lower_left: bfloat16 [131072, 32], P(('grp', 'blk')), may hold values from -0.375 to 0.375
- lower_right: bfloat16 [131072, 32], P(('grp', 'blk')), may hold values from -0.03125 to 0.03125
- upper_left: bfloat16 [131072, 32], P(('grp', 'blk')), may hold values from -0.375 to 0.375
- upper_right: bfloat16 [131072, 32], P(('grp', 'blk')), may hold values from -0.03125 to 0.03125
- ranks: int32 [128], P(('grp', 'blk')), may hold values from 8 to 32
- areas: float32 [131072], P(('grp', 'blk')), may hold values from 0.0013810679 to 0.011048543
Outputs:
- potentials: bfloat16 [131072, 256], P(('grp', 'blk'), 'side')
- added_mass: float32 [256, 256], P(('grp', 'blk'), 'side')
The draws below stay inside these ranges and needn't reach their ends.
Inputs may be any that keep to these rules, and one draw needn't show every extreme that they name: In each column d the counts sum to 1024, and every column holds one count equal to 12.
All inputs are finite; a program needn't handle non-finite values.
Results may differ from the reference program's by a relative error of at most 0.0049.
Values may be sent and summed in bfloat16 or wider, within the bound.
No kernel may reach another device: no remote copies, remote signals or barrier semaphores. Data moves between devices by JAX's collectives and lax.ppermute only.
A program may use at most 64 MiB of HBM per device.

```python
import math
import jax
import jax.numpy as jnp
from jax import lax

MODES = 256
R = 32
PB = 1024
NODES_DEV = 1024
PANEL_DEVS = 128
PANELS = 131072
CAP = 12
SLOTS = 196608
SHELL_NODES = 131072


def draw_inverse_diag(key, part):
    key_one, key_two = jax.random.split(jax.random.fold_in(key, 101))
    diagonal = jax.random.uniform(key_one, (PANELS, 1), jnp.float32, 0.6, 1.4)
    off_terms = jax.random.normal(key_two, (PANELS, PB), jnp.float32) * (0.4 / jnp.sqrt(PB * 1.0))
    row_ids = lax.broadcasted_iota(jnp.int32, (PANELS, PB), 0) % PB
    col_ids = lax.broadcasted_iota(jnp.int32, (PANELS, PB), 1)
    return jnp.where(row_ids == col_ids, diagonal, off_terms).astype(jnp.bfloat16)


def draw_counts(key, part):

    def draw_column(column_id):
        column_key = jax.random.fold_in(jax.random.fold_in(key, 202), column_id)
        key_one, key_two = jax.random.split(column_key)
        forced_row = jax.random.randint(key_one, (), 0, PANEL_DEVS)
        ranking = jax.random.permutation(key_two, (PANEL_DEVS - 1) * CAP)
        picked = (ranking < PB - CAP).astype(jnp.int32).reshape(PANEL_DEVS - 1, CAP).sum(axis=1)
        sources = jnp.arange(PANEL_DEVS, dtype=jnp.int32)
        moved = jnp.clip(jnp.where(sources > forced_row, sources - 1, sources), 0, PANEL_DEVS - 2)
        return jnp.where(sources == forced_row, CAP, picked[moved]).astype(jnp.int32)
    columns = jax.vmap(draw_column)(jnp.arange(PANEL_DEVS, dtype=jnp.int32))
    return columns.T.astype(jnp.int32)


def with_ends(entries, stream_key, least, high):
    spot = [jax.random.randint(jax.random.fold_in(stream_key, axis), (), 0, length) for axis, length in enumerate(entries.shape)]
    widest = entries.shape.index(max(entries.shape))
    next_to = spot[:widest] + [(spot[widest] + 1) % entries.shape[widest]] + spot[widest + 1:]
    return entries.at[tuple(spot)].set(least).at[tuple(next_to)].set(high)


def block_levels(key, extent, shards, smallest, top_value):
    loudness, own = 1.0, jax.random.fold_in(key, 6)
    for dim, blocks in shards:
        draws = jnp.exp(jax.random.uniform(jax.random.fold_in(own, dim), (blocks,), jnp.float32, smallest / len(shards), top_value / len(shards)))
        loudness = loudness * jnp.repeat(draws, extent[dim] // blocks).reshape([-1 if axis == dim else 1 for axis in range(len(extent))])
    return loudness


def normal_values(stream_key, dims, scale, limit, pieces=(), held_as=jnp.bfloat16):
    entries = jax.random.normal(stream_key, dims, jnp.float32) * scale
    if len(pieces) > 0:
        entries = block_levels(stream_key, dims, pieces, -0.22, 0.18) * entries
    return jnp.clip(entries, min=-limit, max=limit).astype(held_as)


def setup_inputs(seed: int = 0) -> dict:
    splits = jax.random.split(jax.random.key(seed), 13)
    return {
        "node_modes": normal_values(splits[0], (3, SHELL_NODES, MODES), 1.0, 6.0, ((1, 128), (2, 2))),
        "node_index": with_ends(jax.random.randint(splits[1], (4, SLOTS), 0, NODES_DEV), jax.random.fold_in(splits[1], 1), 0, NODES_DEV - 1).astype(jnp.int32),
        "interp": jnp.clip(0.1 + 0.9 * jax.random.uniform(splits[2], (4, SLOTS), jnp.float32) ** block_levels(splits[2], (4, SLOTS), ((1, 128),), -0.2, 0.2), 0.1, 1.0),
        "normals": normal_values(splits[3], (3, SLOTS), 1.0, 6.0, ((1, 128),), jnp.float32),
        "counts": draw_counts(jax.random.fold_in(splits[12], 71), 0),
        "inverse_diag": draw_inverse_diag(jax.random.fold_in(splits[12], 71), 0),
        "lower_left": normal_values(splits[6], (PANELS, R), (PB // 4) ** -0.5, 0.375, ((0, 128),)),
        "lower_right": normal_values(splits[7], (PANELS, R), (PB * PANEL_DEVS // 4) ** -0.5, 0.03125, ((0, 128),)),
        "upper_left": normal_values(splits[8], (PANELS, R), (PB // 4) ** -0.5, 0.375, ((0, 128),)),
        "upper_right": normal_values(splits[9], (PANELS, R), (PB * PANEL_DEVS // 4) ** -0.5, 0.03125, ((0, 128),)),
        "ranks": with_ends(jax.random.randint(splits[10], (PANEL_DEVS,), R // 4, R + 1), jax.random.fold_in(splits[10], 1), R // 4, R).astype(jnp.int32),
        "areas": jnp.clip(jnp.exp(math.log(0.011048543) - 2.0794415 * jax.random.uniform(splits[11], (PANELS,), jnp.float32) ** block_levels(splits[11], (PANELS,), ((0, 128),), -0.2, 0.2)), 0.0013810679, 0.011048543),
    }


HIGH = lax.Precision.HIGHEST


def shell_rows(node_modes, node_index, interp, normals, source_id):
    span = PANEL_DEVS * CAP
    local_modes = lax.dynamic_slice_in_dim(node_modes, source_id * NODES_DEV, NODES_DEV, 1)
    start_slot = source_id * span
    local_index = lax.dynamic_slice_in_dim(node_index, start_slot, span, 1)
    local_interp = lax.dynamic_slice_in_dim(interp, start_slot, span, 1)
    local_normals = lax.dynamic_slice_in_dim(normals, start_slot, span, 1)
    velocity = jnp.zeros((span, MODES), jnp.float32)
    for corner in range(4):
        picked = jnp.take(local_modes, local_index[corner], axis=1)
        for axis_id in range(3):
            weight_now = local_interp[corner] * local_normals[axis_id]
            velocity = velocity + weight_now[:, None] * picked[axis_id].astype(jnp.float32)
    return velocity.astype(jnp.bfloat16)


def reference(node_modes, node_index, interp, normals, counts, inverse_diag, lower_left, lower_right, upper_left, upper_right, ranks, areas):
    source_ids = jnp.arange(PANEL_DEVS, dtype=jnp.int32)
    velocity = lax.map(lambda source_id: shell_rows(node_modes, node_index, interp, normals, source_id), source_ids)
    velocity = velocity.reshape(PANEL_DEVS, PANEL_DEVS, CAP, MODES)

    def place(block_id):
        column = counts[:, block_id]
        cum_ends = jnp.cumsum(column).astype(jnp.int32)
        cum_starts = cum_ends - column
        position = jnp.arange(PB, dtype=jnp.int32)
        owner = jnp.sum((cum_ends[None, :] <= position[:, None]).astype(jnp.int32), axis=1)
        slot_pos = position - cum_starts[owner]
        return velocity[owner, block_id, slot_pos]

    normal_velocity = lax.map(place, source_ids)
    mask_cols = jnp.arange(R, dtype=jnp.int32)

    def forward(carried, inputs):
        inverse_block, left_block, right_block, rank_now, rhs_block = inputs
        keep = (mask_cols < rank_now)[None, :]
        left_masked = jnp.where(keep, left_block, jnp.zeros_like(left_block))
        solved = jnp.dot(inverse_block, rhs_block, preferred_element_type=jnp.float32)
        spread = jnp.dot(inverse_block, left_masked, preferred_element_type=jnp.float32)
        interim = solved - jnp.dot(spread, carried, precision=HIGH)
        carried = carried + jnp.dot(right_block.astype(jnp.float32).T, interim, precision=HIGH)
        return carried, interim

    inputs = (inverse_diag.reshape(PANEL_DEVS, PB, PB), lower_left.reshape(PANEL_DEVS, PB, R), lower_right.reshape(PANEL_DEVS, PB, R), ranks, normal_velocity)
    ignored, interim = lax.scan(forward, jnp.zeros((R, MODES), jnp.float32), inputs)

    def backward(carried, inputs):
        left_block, right_block, rank_now, interim_block = inputs
        keep = (mask_cols < rank_now)[None, :]
        left_masked = jnp.where(keep, left_block, jnp.zeros_like(left_block)).astype(jnp.float32)
        result = interim_block - jnp.dot(left_masked, carried, precision=HIGH)
        carried = carried + jnp.dot(right_block.astype(jnp.float32).T, result, precision=HIGH)
        return carried, result

    inputs = (upper_left.reshape(PANEL_DEVS, PB, R), upper_right.reshape(PANEL_DEVS, PB, R), ranks, interim)
    ignored, result = lax.scan(backward, jnp.zeros((R, MODES), jnp.float32), inputs, reverse=True)
    potentials = result.reshape(PANELS, MODES).astype(jnp.bfloat16)
    weighted = (areas[:, None] * potentials.astype(jnp.float32)).astype(jnp.bfloat16)
    flat_velocity = normal_velocity.reshape(PANELS, MODES)
    added_mass = jnp.dot(flat_velocity.T, weighted, preferred_element_type=jnp.float32)
    return potentials, added_mass
```

```python
import functools
import jax
import jax.numpy as jnp
from jax import lax
from jax.experimental import pallas as pl
from jax.experimental.pallas import tpu as pltpu
from jax.sharding import PartitionSpec as P

F32, BF16, I32 = jnp.float32, jnp.bfloat16, jnp.int32
AXES = ("y", "x", "z")
RANK, CAP, SLOT_ROWS, WIDE = 32, 12, 16, 256
PARAMS = pltpu.CompilerParams(vmem_limit_bytes=28 * 1024 * 1024)
VMEM = pl.BlockSpec(memory_space=pltpu.VMEM)
SMEM = pl.BlockSpec(memory_space=pltpu.SMEM)


def mm(a, b):
    return lax.dot_general(a, b, (((1,), (0,)), ((), ())), preferred_element_type=F32)


def mm_t(a, b):
    return lax.dot_general(a, b, (((1,), (1,)), ((), ())), preferred_element_type=F32)


def halves(value):
    high = value.astype(BF16)
    return high, (value - high.astype(F32)).astype(BF16)


def tall(value):
    high, low = halves(value)
    return jnp.concatenate([high, high, low], axis=0)


def interp_kernel(modes_ref, index_ref, interp_ref, normals_ref, out_ref):
    chunk = index_ref.shape[1]
    nodes = modes_ref.shape[1]
    rows = jnp.concatenate(
        [
            index_ref[...].astype(F32),
            interp_ref[...],
            normals_ref[...],
            jnp.zeros((5, chunk), F32),
        ],
        axis=0,
    )
    columns = rows.T
    node = lax.broadcasted_iota(I32, (chunk, nodes), 1).astype(F32)
    mix = jnp.zeros((chunk, nodes), F32)
    for corner in range(4):
        here = columns[:, corner : corner + 1] == node
        mix = mix + jnp.where(here, columns[:, 4 + corner : 5 + corner], 0.0)
    table = jnp.concatenate([modes_ref[0], modes_ref[1], modes_ref[2]], axis=1)
    high, low = halves(mix)
    picked = mm(high, table) + mm(low, table)
    width = modes_ref.shape[2]
    velocity = jnp.zeros((chunk, width), F32)
    for axis_id in range(3):
        part = picked[:, axis_id * width : (axis_id + 1) * width]
        velocity = velocity + columns[:, 8 + axis_id : 9 + axis_id] * part
    pairs = velocity.reshape(chunk // 24, 24, width)
    out_ref[:, 0:16, :] = pairs[:, 0:16, :].astype(BF16)
    out_ref[:, 16:32, :] = pairs[:, 8:24, :].astype(BF16)


def interpolate(node_modes, node_index, interp, normals):
    slots, width = node_index.shape[1], node_modes.shape[2]
    steps = 4
    chunk = slots // steps
    return pl.pallas_call(
        interp_kernel,
        grid=(steps,),
        in_specs=[
            pl.BlockSpec(node_modes.shape, lambda i: (0, 0, 0)),
            pl.BlockSpec((4, chunk), lambda i: (0, i)),
            pl.BlockSpec((4, chunk), lambda i: (0, i)),
            pl.BlockSpec((3, chunk), lambda i: (0, i)),
        ],
        out_specs=pl.BlockSpec((chunk // 24, 32, width), lambda i: (i, 0, 0)),
        out_shape=jax.ShapeDtypeStruct((slots // 24, 32, width), BF16),
        compiler_params=PARAMS,
        cost_estimate=pl.CostEstimate(
            flops=2 * slots * 1024 * 384, bytes_accessed=1 << 20, transcendentals=0
        ),
    )(node_modes, node_index, interp, normals)


def prepare_kernel(
    place_ref, rank_ref, count_ref, diag_ref, lower_ref, right_ref, upper_ref, back_ref,
    stack_ref, mats_ref, target_ref,
):
    panels = diag_ref.shape[0]
    keep = lax.broadcasted_iota(I32, (RANK, panels), 0) < rank_ref[0]
    zero = jnp.zeros((RANK, panels), BF16)
    lower = jnp.where(keep, lower_ref[...], zero)
    upper = jnp.where(keep, upper_ref[...], zero)
    spread = mm_t(diag_ref[...], lower)
    high, low = halves(spread)
    both = jnp.concatenate([right_ref[...], back_ref[...]], axis=0)
    seen = mm(both, jnp.concatenate([high, low], axis=1))
    seen = seen[:, :RANK] + seen[:, RANK:]
    back = mm_t(back_ref[...], upper)
    blank = jnp.zeros((RANK, RANK), F32)
    mats = jnp.concatenate([-seen[:RANK], -back, seen[RANK:], blank], axis=1)
    mats_high, mats_low = halves(mats)
    mats_ref[...] = jnp.concatenate([mats_high, mats_low], axis=0)
    stack_ref[...] = jnp.concatenate(
        [high, upper.astype(F32).T.astype(BF16), low, jnp.zeros((panels, RANK), BF16)], axis=1
    )
    sources = count_ref.shape[1]
    slots = target_ref.shape[1]
    counts = jnp.broadcast_to(count_ref[...].astype(F32), (16, sources)).astype(BF16)
    source = lax.broadcasted_iota(I32, (sources, slots), 0)
    column = lax.broadcasted_iota(I32, (sources, slots), 1) // SLOT_ROWS
    start = mm(counts, jnp.where(source < column, 1.0, 0.0).astype(BF16))[0:1]
    mine = mm(counts, jnp.where(source == column, 1.0, 0.0).astype(BF16))[0:1]
    slot = lax.broadcasted_iota(I32, (1, slots), 1) % SLOT_ROWS - 4 * place_ref[3]
    slot = slot.astype(F32)
    target_ref[...] = jnp.where((slot >= 0.0) & (slot < mine), start + slot, -1.0)


def prepare(place, rank, count, diag, lower, right, upper, back):
    panels, slots = diag.shape[0], count.shape[1] * SLOT_ROWS
    return pl.pallas_call(
        prepare_kernel,
        in_specs=[SMEM, SMEM] + [VMEM] * 6,
        out_specs=[VMEM] * 3,
        out_shape=[
            jax.ShapeDtypeStruct((panels, 4 * RANK), BF16),
            jax.ShapeDtypeStruct((2 * RANK, 4 * RANK), BF16),
            jax.ShapeDtypeStruct((1, slots), F32),
        ],
        compiler_params=PARAMS,
        cost_estimate=pl.CostEstimate(
            flops=4 << 30, bytes_accessed=8 << 20, transcendentals=0
        ),
    )(place, rank, count, diag, lower, right, upper, back)


def solve_kernel(
    arrived_ref, target_ref, diag_ref, right_ref, back_ref, mats_ref,
    solved_ref, turned_ref, send_ref,
):
    panels = diag_ref.shape[0]
    slots = target_ref.shape[1]
    step = 256
    target = target_ref[...]
    arrived = arrived_ref[...]
    parts = []
    for begin in range(0, panels, step):
        panel = (lax.broadcasted_iota(I32, (step, slots), 0) + begin).astype(F32)
        pick = jnp.where(panel == target, 1.0, 0.0).astype(BF16)
        parts.append(mm(pick, arrived))
    normal = jnp.concatenate(parts, axis=0)
    turned_ref[...] = normal.T.astype(BF16)
    solved = mm(diag_ref[...], normal.astype(BF16))
    solved_ref[...] = solved
    high, low = halves(solved)
    width = solved.shape[1]
    both = jnp.concatenate([right_ref[...], back_ref[...]], axis=0)
    seen = mm(both, jnp.concatenate([high, low], axis=1))
    seen = (seen[:, :width] + seen[:, width:]).astype(BF16)
    message = jnp.concatenate([seen, mats_ref[...]], axis=0)
    send_ref[...] = jnp.broadcast_to(message[None], send_ref.shape)


def solve(arrived, target, diag, right, back, mats, peers):
    panels, width = diag.shape[0], arrived.shape[1]
    return pl.pallas_call(
        solve_kernel,
        in_specs=[VMEM] * 6,
        out_specs=[VMEM] * 3,
        out_shape=[
            jax.ShapeDtypeStruct((panels, width), F32),
            jax.ShapeDtypeStruct((width, panels), BF16),
            jax.ShapeDtypeStruct((peers, 4 * RANK, width), BF16),
        ],
        compiler_params=PARAMS,
        cost_estimate=pl.CostEstimate(
            flops=1 << 30, bytes_accessed=4 << 20, transcendentals=0
        ),
    )(arrived, target, diag, right, back, mats)


def element(ref, position):
    high = ref[position, 2 * RANK : 3 * RANK, :]
    low = ref[position, 3 * RANK : 4 * RANK, :]

    def wide(which):
        lanes = slice(which * RANK, (which + 1) * RANK)
        return jnp.concatenate([high[:, lanes], low[:, lanes], high[:, lanes]], axis=1)

    vectors = ref[position, 0 : 2 * RANK, :].astype(F32)
    ahead = jnp.concatenate([wide(0), wide(2)], axis=0)
    return vectors[:RANK], vectors[RANK:], ahead, wide(1)


def chain(ref, mine, first, last, lift):
    count = ref.shape[0]
    elements = [element(ref, position) for position in range(count)]
    forward, own_forward, given = first, jnp.zeros_like(first), []
    for position in range(count):
        shift, gain, ahead, _ = elements[position]
        own_forward = jnp.where(mine == position, forward, own_forward)
        moved = mm(ahead, tall(forward))
        given.append(lift(gain) - moved[RANK:])
        forward = forward + moved[:RANK] + lift(shift)
    backward, own_backward = last, jnp.zeros_like(last)
    for position in reversed(range(count)):
        own_backward = jnp.where(mine == position, backward, own_backward)
        backward = backward + mm(elements[position][3], tall(backward)) + given[position]
    return forward, backward, own_forward, own_backward


def unit(offset):
    row = lax.broadcasted_iota(I32, (RANK, WIDE), 0)
    lane = lax.broadcasted_iota(I32, (RANK, WIDE), 1)
    return jnp.where(lane == row + offset, 1.0, 0.0).astype(F32)


def inner_kernel(place_ref, got_ref, own_ref, send_ref):
    width = got_ref.shape[2]
    pad = jnp.zeros((RANK, WIDE - width), F32)
    lift = lambda value: jnp.concatenate([value, pad], axis=1)
    in_t, in_s = width, width + RANK
    forward, backward, own_s, own_t = chain(
        got_ref, place_ref[0], unit(in_s), unit(in_t), lift
    )
    own_ref[...] = jnp.concatenate([own_s, own_t], axis=0)
    eye = unit(0)[:, :RANK]
    mats = jnp.concatenate(
        [
            forward[:, in_s : in_s + RANK] - eye,
            backward[:, in_t : in_t + RANK] - eye,
            -backward[:, in_s : in_s + RANK],
            jnp.zeros((RANK, RANK), F32),
        ],
        axis=1,
    )
    high, low = halves(mats)
    message = jnp.concatenate(
        [forward[:, :width].astype(BF16), backward[:, :width].astype(BF16), high, low], axis=0
    )
    send_ref[...] = jnp.broadcast_to(message[None], send_ref.shape)


def inner(place, got, peers):
    return pl.pallas_call(
        inner_kernel,
        in_specs=[SMEM, VMEM],
        out_specs=[VMEM] * 2,
        out_shape=[
            jax.ShapeDtypeStruct((2 * RANK, WIDE), F32),
            jax.ShapeDtypeStruct((peers,) + got.shape[1:], BF16),
        ],
        compiler_params=PARAMS,
    )(place, got)


def outer_kernel(
    place_ref, got_ref, own_ref, solved_ref, stack_ref, turned_ref, other_ref, area_ref,
    potential_ref, mass_ref,
):
    width = got_ref.shape[2]
    panels = solved_ref.shape[0]
    zero = jnp.zeros((RANK, width), F32)
    _, _, in_s, in_t = chain(got_ref, place_ref[1], zero, zero, lambda value: value)
    own = own_ref[...]
    map_high, map_low = halves(own[:, width : width + 2 * RANK])
    maps = jnp.concatenate([map_high, map_low, map_high], axis=1)
    state = own[:, :width] + mm(maps, tall(jnp.concatenate([in_t, in_s], axis=0)))
    high, low = halves(state)
    blank = jnp.zeros((RANK, width), BF16)
    left = jnp.concatenate([high, high[:RANK], blank], axis=0)
    right = jnp.concatenate([low, blank, blank], axis=0)
    fixed = mm(stack_ref[...], jnp.concatenate([left, right], axis=1))
    potential = (solved_ref[...] - (fixed[:, :width] + fixed[:, width:])).astype(BF16)
    potential_ref[...] = potential
    area = jnp.broadcast_to(area_ref[...], (8, panels)).T[:, 0:1]
    weighted = (area * potential.astype(F32)).astype(BF16)
    side = place_ref[2]
    mass_ref[pl.ds(pl.multiple_of(side * width, width), width), :] = mm(turned_ref[...], weighted)
    mass_ref[pl.ds(pl.multiple_of((1 - side) * width, width), width), :] = mm(
        other_ref[...], weighted
    )


def outer(place, got, own, solved, stack, turned, other, area):
    panels, width = solved.shape
    return pl.pallas_call(
        outer_kernel,
        in_specs=[SMEM] + [VMEM] * 7,
        out_specs=[VMEM] * 2,
        out_shape=[
            jax.ShapeDtypeStruct((panels, width), BF16),
            jax.ShapeDtypeStruct((2 * width, width), F32),
        ],
        compiler_params=PARAMS,
    )(place, got, own, solved, stack, turned, other, area)


def body(
    node_modes, node_index, interp, normals, counts, inverse_diag,
    lower_left, lower_right, upper_left, upper_right, ranks, areas,
):
    devices, width = lax.axis_size(AXES), node_modes.shape[2]
    inner_size, outer_size = lax.axis_size("z"), lax.axis_size(("y", "x"))
    depth, group = lax.axis_index("z"), lax.axis_index(("y", "x"))
    place = jnp.stack([depth, group, lax.axis_index("side"), depth % 2]).astype(I32)
    outgoing = interpolate(node_modes, node_index, interp, normals)
    arrived = lax.all_to_all(
        outgoing.reshape(devices, SLOT_ROWS, width), AXES, split_axis=0, concat_axis=0, tiled=True
    ).reshape(devices * SLOT_ROWS, width)
    right, back = lower_right.T, upper_right.T
    stack, mats, target = prepare(
        place, ranks, counts.reshape(1, devices), inverse_diag, lower_left.T, right,
        upper_left.T, back,
    )
    solved, turned, send = solve(
        arrived, target, inverse_diag, right, back, mats, inner_size
    )
    other = lax.ppermute(turned, "side", [(0, 1), (1, 0)])
    got = lax.all_to_all(send, "z", split_axis=0, concat_axis=0, tiled=True)
    own, send = inner(place, got, outer_size)
    got = lax.all_to_all(send, ("y", "x"), split_axis=0, concat_axis=0, tiled=True)
    potentials, mass = outer(
        place, got, own, solved, stack, turned, other, areas.reshape(1, -1)
    )
    rows = mass.shape[0] // devices
    pieces = lax.all_to_all(
        mass.reshape(devices, rows, width), AXES, split_axis=0, concat_axis=0, tiled=True
    )
    return potentials, jnp.sum(pieces, axis=0)


def solution(mesh):
    grid = jax.sharding.Mesh(mesh.devices.reshape(2, 4, 4, 8), ("side",) + AXES)
    in_specs = (
        P(None, AXES, "side"),
        P(None, AXES),
        P(None, AXES),
        P(None, AXES),
        P(None, AXES),
        P(AXES, None),
        P(AXES, None),
        P(AXES, None),
        P(AXES, None),
        P(AXES, None),
        P(AXES),
        P(AXES),
    )
    out_specs = (P(AXES, "side"), P(AXES, "side"))
    return jax.shard_map(body, mesh=grid, in_specs=in_specs, out_specs=out_specs, check_vma=False)
```

```python
import functools
import jax
import jax.numpy as jnp
from jax import lax
from jax.experimental import pallas as pl
from jax.experimental.pallas import tpu as pltpu
from jax.sharding import PartitionSpec as P

F32, BF16, I32 = jnp.float32, jnp.bfloat16, jnp.int32
AXES = ("y", "x", "z")
RANK, CAP, SLOT_ROWS, WIDE = 32, 12, 16, 256
PARAMS = pltpu.CompilerParams(vmem_limit_bytes=28 * 1024 * 1024)
WHOLE = pltpu.CompilerParams(vmem_limit_bytes=62 * 1024 * 1024)
LARGE = pltpu.CompilerParams(vmem_limit_bytes=103 * 512 * 1024)
VMEM = pl.BlockSpec(memory_space=pltpu.VMEM)
SMEM = pl.BlockSpec(memory_space=pltpu.SMEM)
HBM = pl.BlockSpec(memory_space=pltpu.HBM)
STEPS, TURN = 4, 128


def mm(a, b):
    return lax.dot_general(a, b, (((1,), (0,)), ((), ())), preferred_element_type=F32)


def mm_t(a, b):
    return lax.dot_general(a, b, (((1,), (1,)), ((), ())), preferred_element_type=F32)


def halves(value):
    high = value.astype(BF16)
    return high, (value - high.astype(F32)).astype(BF16)


def tall(value):
    high, low = halves(value)
    return jnp.concatenate([high, high, low], axis=0)


def interp_kernel(
    modes_hbm, index_hbm, interp_hbm, normals_hbm, out_ref,
    modes_ref, index_ref, interp_ref, normals_ref, sems,
):
    pairs = [
        (index_hbm, index_ref), (interp_hbm, interp_ref), (normals_hbm, normals_ref),
        (modes_hbm, modes_ref),
    ]
    copies = [
        pltpu.make_async_copy(source, target, sems.at[number])
        for number, (source, target) in enumerate(pairs)
    ]
    for copy in copies:
        copy.start()
    for copy in copies[:3]:
        copy.wait()
    slots, nodes = index_ref.shape[1], modes_ref.shape[1]
    width = modes_ref.shape[2]
    chunk = slots // STEPS
    node = lax.broadcasted_iota(I32, (chunk, nodes), 1).astype(F32)
    for step in range(STEPS):
        lanes = slice(step * chunk, (step + 1) * chunk)
        rows = jnp.concatenate(
            [
                index_ref[:, lanes].astype(F32),
                interp_ref[:, lanes],
                normals_ref[:, lanes],
                jnp.zeros((5, chunk), F32),
            ],
            axis=0,
        )
        columns = rows.T
        mix = jnp.zeros((chunk, nodes), F32)
        for corner in range(4):
            here = columns[:, corner : corner + 1] == node
            mix = mix + jnp.where(here, columns[:, 4 + corner : 5 + corner], 0.0)
        high, low = halves(mix)
        if step == 0:
            copies[3].wait()
        table = jnp.concatenate([modes_ref[0], modes_ref[1], modes_ref[2]], axis=1)
        picked = mm(high, table) + mm(low, table)
        velocity = jnp.zeros((chunk, width), F32)
        for axis_id in range(3):
            part = picked[:, axis_id * width : (axis_id + 1) * width]
            velocity = velocity + columns[:, 8 + axis_id : 9 + axis_id] * part
        blocks = velocity.reshape(chunk // 24, 24, width)
        where = slice(step * chunk // 24, (step + 1) * chunk // 24)
        out_ref[where, 0:16, :] = blocks[:, 0:16, :].astype(BF16)
        out_ref[where, 16:32, :] = blocks[:, 8:24, :].astype(BF16)


def interpolate(node_modes, node_index, interp, normals):
    slots, width = node_index.shape[1], node_modes.shape[2]
    return pl.pallas_call(
        interp_kernel,
        in_specs=[HBM] * 4,
        out_specs=VMEM,
        out_shape=jax.ShapeDtypeStruct((slots // 24, 32, width), BF16),
        scratch_shapes=[
            pltpu.VMEM(node_modes.shape, BF16),
            pltpu.VMEM(node_index.shape, I32),
            pltpu.VMEM(interp.shape, F32),
            pltpu.VMEM(normals.shape, F32),
            pltpu.SemaphoreType.DMA((4,)),
        ],
        compiler_params=WHOLE,
        cost_estimate=pl.CostEstimate(
            flops=2 * slots * 1024 * 384, bytes_accessed=1 << 20, transcendentals=0
        ),
    )(node_modes, node_index, interp, normals)


def prepare_kernel(
    place_ref, rank_ref, count_ref, diag_ref, lower_ref, right_ref, upper_ref, back_ref,
    stack_ref, mats_ref, target_ref,
):
    panels = diag_ref.shape[0]
    keep = lax.broadcasted_iota(I32, (RANK, panels), 0) < rank_ref[0]
    zero = jnp.zeros((RANK, panels), BF16)
    lower = jnp.where(keep, lower_ref[...], zero)
    upper = jnp.where(keep, upper_ref[...], zero)
    spread = mm_t(diag_ref[...], lower)
    high, low = halves(spread)
    both = jnp.concatenate([right_ref[...], back_ref[...]], axis=0)
    seen = mm(both, jnp.concatenate([high, low], axis=1))
    seen = seen[:, :RANK] + seen[:, RANK:]
    back = mm_t(back_ref[...], upper)
    blank = jnp.zeros((RANK, RANK), F32)
    mats = jnp.concatenate([-seen[:RANK], -back, seen[RANK:], blank], axis=1)
    mats_high, mats_low = halves(mats)
    mats_ref[...] = jnp.concatenate([mats_high, mats_low], axis=0)
    stack_ref[...] = jnp.concatenate(
        [high, upper.astype(F32).T.astype(BF16), low, jnp.zeros((panels, RANK), BF16)], axis=1
    )
    sources = count_ref.shape[1]
    slots = target_ref.shape[1]
    counts = jnp.broadcast_to(count_ref[...].astype(F32), (16, sources)).astype(BF16)
    source = lax.broadcasted_iota(I32, (sources, slots), 0)
    column = lax.broadcasted_iota(I32, (sources, slots), 1) // SLOT_ROWS
    start = mm(counts, jnp.where(source < column, 1.0, 0.0).astype(BF16))[0:1]
    mine = mm(counts, jnp.where(source == column, 1.0, 0.0).astype(BF16))[0:1]
    slot = lax.broadcasted_iota(I32, (1, slots), 1) % SLOT_ROWS - 4 * place_ref[3]
    slot = slot.astype(F32)
    target_ref[...] = jnp.where((slot >= 0.0) & (slot < mine), start + slot, -1.0)


def prepare(place, rank, count, diag, lower, right, upper, back):
    panels, slots = diag.shape[0], count.shape[1] * SLOT_ROWS
    return pl.pallas_call(
        prepare_kernel,
        in_specs=[SMEM, SMEM] + [VMEM] * 6,
        out_specs=[VMEM] * 3,
        out_shape=[
            jax.ShapeDtypeStruct((panels, 4 * RANK), BF16),
            jax.ShapeDtypeStruct((2 * RANK, 4 * RANK), BF16),
            jax.ShapeDtypeStruct((1, slots), F32),
        ],
        compiler_params=PARAMS,
        cost_estimate=pl.CostEstimate(
            flops=4 << 30, bytes_accessed=8 << 20, transcendentals=0
        ),
    )(place, rank, count, diag, lower, right, upper, back)


def solve_kernel(
    arrived_ref, target_ref, diag_hbm, right_ref, back_ref, mats_ref,
    solved_ref, turned_ref, send_ref, diag_ref, sem,
):
    fetch = pltpu.make_async_copy(diag_hbm, diag_ref, sem)
    fetch.start()
    panels = diag_ref.shape[0]
    slots = target_ref.shape[1]
    step = 256
    target = target_ref[...]
    arrived = arrived_ref[...]
    parts = []
    for begin in range(0, panels, step):
        panel = (lax.broadcasted_iota(I32, (step, slots), 0) + begin).astype(F32)
        pick = jnp.where(panel == target, 1.0, 0.0).astype(BF16)
        parts.append(mm(pick, arrived))
    normal = jnp.concatenate(parts, axis=0)
    turned_ref[...] = normal.T.astype(BF16)
    fetch.wait()
    solved = mm(diag_ref[...], normal.astype(BF16))
    solved_ref[...] = solved
    high, low = halves(solved)
    width = solved.shape[1]
    both = jnp.concatenate([right_ref[...], back_ref[...]], axis=0)
    seen = mm(both, jnp.concatenate([high, low], axis=1))
    seen = (seen[:, :width] + seen[:, width:]).astype(BF16)
    message = jnp.concatenate([seen, mats_ref[...]], axis=0)
    send_ref[...] = jnp.broadcast_to(message[None], send_ref.shape)


def solve(arrived, target, diag, right, back, mats, peers):
    panels, width = diag.shape[0], arrived.shape[1]
    return pl.pallas_call(
        solve_kernel,
        in_specs=[VMEM, VMEM, HBM, VMEM, VMEM, VMEM],
        out_specs=[VMEM] * 3,
        scratch_shapes=[pltpu.VMEM(diag.shape, BF16), pltpu.SemaphoreType.DMA],
        out_shape=[
            jax.ShapeDtypeStruct((panels, width), F32),
            jax.ShapeDtypeStruct((width, panels), BF16),
            jax.ShapeDtypeStruct((peers, 4 * RANK, width), BF16),
        ],
        compiler_params=LARGE,
        cost_estimate=pl.CostEstimate(
            flops=1 << 30, bytes_accessed=4 << 20, transcendentals=0
        ),
    )(arrived, target, diag, right, back, mats)


def element(ref, position):
    high = ref[position, 2 * RANK : 3 * RANK, :]
    low = ref[position, 3 * RANK : 4 * RANK, :]

    def wide(which):
        lanes = slice(which * RANK, (which + 1) * RANK)
        return jnp.concatenate([high[:, lanes], low[:, lanes], high[:, lanes]], axis=1)

    vectors = ref[position, 0 : 2 * RANK, :].astype(F32)
    ahead = jnp.concatenate([wide(0), wide(2)], axis=0)
    back = high[:, RANK : 2 * RANK].astype(F32) + low[:, RANK : 2 * RANK].astype(F32)
    return vectors[:RANK], vectors[RANK:], ahead, back


def gain_step(total, mask, middle):
    factor = total[:, TURN : TURN + RANK]
    if mask is not None:
        factor = factor * mask
    high, low = halves(factor)
    middle_high, middle_low = halves(middle)
    rows = factor.shape[0]
    first = mm(jnp.concatenate([high, low], axis=0), middle_high)
    return total + (first[:rows] + first[rows:] + mm(high, middle_low))


def unit(offset):
    row = lax.broadcasted_iota(I32, (RANK, WIDE), 0)
    lane = lax.broadcasted_iota(I32, (RANK, WIDE), 1)
    return jnp.where(lane == row + offset, 1.0, 0.0).astype(F32)


def inner_kernel(place_ref, got_ref, own_ref, send_ref):
    width = got_ref.shape[2]
    mine = place_ref[0]
    in_t, in_s = TURN, TURN + RANK
    forward = unit(in_s)
    own_s = jnp.zeros_like(forward)
    total = jnp.concatenate([unit(in_t), unit(in_t)], axis=0)
    pad = jnp.zeros((RANK, WIDE - width), F32)
    gap, tail = jnp.zeros((RANK, width), F32), jnp.zeros((RANK, WIDE - width - RANK), F32)
    row = lax.broadcasted_iota(I32, (2 * RANK, RANK), 0)
    for position in range(got_ref.shape[0]):
        shift, gain, ahead, back = element(got_ref, position)
        own_s = jnp.where(mine == position, forward, own_s)
        moved = mm(ahead, tall(forward))
        forward = forward + moved[:RANK] + jnp.concatenate([shift, pad], axis=1)
        middle = (
            jnp.concatenate([gain, pad], axis=1)
            + jnp.concatenate([gap, back, tail], axis=1)
            - moved[RANK:]
        )
        mask = jnp.where((row < RANK) | (position > mine), 1.0, 0.0)
        total = gain_step(total, mask, middle)
    own_ref[...] = jnp.concatenate([own_s, total[RANK:]], axis=0)
    eye = unit(0)[:, :RANK]
    mats = jnp.concatenate(
        [
            forward[:, in_s : in_s + RANK] - eye,
            total[:RANK, in_t : in_t + RANK] - eye,
            -total[:RANK, in_s : in_s + RANK],
            jnp.zeros((RANK, RANK), F32),
        ],
        axis=1,
    )
    high, low = halves(mats)
    message = jnp.concatenate(
        [forward[:, :width].astype(BF16), total[:RANK, :width].astype(BF16), high, low], axis=0
    )
    send_ref[...] = jnp.broadcast_to(message[None], send_ref.shape)


def inner(place, got, peers):
    return pl.pallas_call(
        inner_kernel,
        in_specs=[SMEM, VMEM],
        out_specs=[VMEM] * 2,
        out_shape=[
            jax.ShapeDtypeStruct((2 * RANK, WIDE), F32),
            jax.ShapeDtypeStruct((peers,) + got.shape[1:], BF16),
        ],
        compiler_params=PARAMS,
    )(place, got)


def outer_kernel(
    place_ref, got_ref, own_ref, solved_ref, stack_ref, turned_ref, other_ref, area_ref,
    potential_ref, mass_ref,
):
    width = got_ref.shape[2]
    panels = solved_ref.shape[0]
    mine = place_ref[1]
    forward = jnp.zeros((RANK, width), F32)
    in_s, total = forward, unit(TURN)
    rest = jnp.zeros((RANK, WIDE - width - RANK), F32)
    for position in range(got_ref.shape[0]):
        shift, gain, ahead, back = element(got_ref, position)
        in_s = jnp.where(mine == position, forward, in_s)
        moved = mm(ahead, tall(forward))
        forward = forward + moved[:RANK] + shift
        middle = jnp.concatenate([gain - moved[RANK:], back, rest], axis=1)
        total = gain_step(total, jnp.where(position > mine, 1.0, 0.0), middle)
    in_t = total[:, :width]
    own = own_ref[...]
    map_high, map_low = halves(own[:, width : width + 2 * RANK])
    maps = jnp.concatenate([map_high, map_low, map_high], axis=1)
    state = own[:, :width] + mm(maps, tall(jnp.concatenate([in_t, in_s], axis=0)))
    high, low = halves(state)
    blank = jnp.zeros((RANK, width), BF16)
    left = jnp.concatenate([high, high[:RANK], blank], axis=0)
    right = jnp.concatenate([low, blank, blank], axis=0)
    fixed = mm(stack_ref[...], jnp.concatenate([left, right], axis=1))
    potential = (solved_ref[...] - (fixed[:, :width] + fixed[:, width:])).astype(BF16)
    potential_ref[...] = potential
    area = jnp.broadcast_to(area_ref[...], (8, panels)).T[:, 0:1]
    weighted = (area * potential.astype(F32)).astype(BF16)
    side = place_ref[2]
    mass_ref[pl.ds(pl.multiple_of(side * width, width), width), :] = mm(turned_ref[...], weighted)
    mass_ref[pl.ds(pl.multiple_of((1 - side) * width, width), width), :] = mm(
        other_ref[...], weighted
    )


def outer(place, got, own, solved, stack, turned, other, area):
    panels, width = solved.shape
    return pl.pallas_call(
        outer_kernel,
        in_specs=[SMEM] + [VMEM] * 7,
        out_specs=[VMEM] * 2,
        out_shape=[
            jax.ShapeDtypeStruct((panels, width), BF16),
            jax.ShapeDtypeStruct((2 * width, width), F32),
        ],
        compiler_params=PARAMS,
    )(place, got, own, solved, stack, turned, other, area)


def body(
    node_modes, node_index, interp, normals, counts, inverse_diag,
    lower_left, lower_right, upper_left, upper_right, ranks, areas,
):
    devices, width = lax.axis_size(AXES), node_modes.shape[2]
    inner_size, outer_size = lax.axis_size("z"), lax.axis_size(("y", "x"))
    depth, group = lax.axis_index("z"), lax.axis_index(("y", "x"))
    place = jnp.stack([depth, group, lax.axis_index("side"), depth % 2]).astype(I32)
    outgoing = interpolate(node_modes, node_index, interp, normals)
    arrived = lax.all_to_all(
        outgoing.reshape(devices, SLOT_ROWS, width), AXES, split_axis=0, concat_axis=0, tiled=True
    ).reshape(devices * SLOT_ROWS, width)
    right, back = lower_right.T, upper_right.T
    stack, mats, target = prepare(
        place, ranks, counts.reshape(1, devices), inverse_diag, lower_left.T, right,
        upper_left.T, back,
    )
    solved, turned, send = solve(
        arrived, target, inverse_diag, right, back, mats, inner_size
    )
    other = lax.ppermute(turned, "side", [(0, 1), (1, 0)])
    got = lax.all_to_all(send, "z", split_axis=0, concat_axis=0, tiled=True)
    own, send = inner(place, got, outer_size)
    got = lax.all_to_all(send, ("y", "x"), split_axis=0, concat_axis=0, tiled=True)
    potentials, mass = outer(
        place, got, own, solved, stack, turned, other, areas.reshape(1, -1)
    )
    rows = mass.shape[0] // devices
    pieces = lax.all_to_all(
        mass.reshape(devices, rows, width), AXES, split_axis=0, concat_axis=0, tiled=True
    )
    return potentials, jnp.sum(pieces, axis=0)


def solution(mesh):
    grid = jax.sharding.Mesh(mesh.devices.reshape(2, 4, 4, 8), ("side",) + AXES)
    in_specs = (
        P(None, AXES, "side"),
        P(None, AXES),
        P(None, AXES),
        P(None, AXES),
        P(None, AXES),
        P(AXES, None),
        P(AXES, None),
        P(AXES, None),
        P(AXES, None),
        P(AXES, None),
        P(AXES),
        P(AXES),
    )
    out_specs = (P(AXES, "side"), P(AXES, "side"))
    return jax.shard_map(body, mesh=grid, in_specs=in_specs, out_specs=out_specs, check_vma=False)
```

```python
import functools
import jax
import jax.numpy as jnp
from jax import lax
from jax.experimental import pallas as pl
from jax.experimental.pallas import tpu as pltpu
from jax.sharding import PartitionSpec as P

F32, BF16, I32 = jnp.float32, jnp.bfloat16, jnp.int32
AXES = ("y", "x", "z")
RANK, CAP, SLOT_ROWS, WIDE = 32, 12, 16, 256
PARAMS = pltpu.CompilerParams(vmem_limit_bytes=28 * 1024 * 1024)
WHOLE = pltpu.CompilerParams(vmem_limit_bytes=62 * 1024 * 1024)
VMEM = pl.BlockSpec(memory_space=pltpu.VMEM)
SMEM = pl.BlockSpec(memory_space=pltpu.SMEM)
HBM = pl.BlockSpec(memory_space=pltpu.HBM)
STEPS, TURN = 4, 128


def mm(a, b):
    return lax.dot_general(a, b, (((1,), (0,)), ((), ())), preferred_element_type=F32)


def mm_t(a, b):
    return lax.dot_general(a, b, (((1,), (1,)), ((), ())), preferred_element_type=F32)


def halves(value):
    high = value.astype(BF16)
    return high, (value - high.astype(F32)).astype(BF16)


def tall(value):
    high, low = halves(value)
    return jnp.concatenate([high, high, low], axis=0)


def interp_kernel(
    modes_hbm, index_hbm, interp_hbm, normals_hbm, out_ref,
    modes_ref, index_ref, interp_ref, normals_ref, sems,
):
    pairs = [
        (index_hbm, index_ref), (interp_hbm, interp_ref), (normals_hbm, normals_ref),
        (modes_hbm, modes_ref),
    ]
    copies = [
        pltpu.make_async_copy(source, target, sems.at[number])
        for number, (source, target) in enumerate(pairs)
    ]
    for copy in copies:
        copy.start()
    for copy in copies[:3]:
        copy.wait()
    slots, nodes = index_ref.shape[1], modes_ref.shape[1]
    width = modes_ref.shape[2]
    chunk = slots // STEPS
    node = lax.broadcasted_iota(I32, (chunk, nodes), 1).astype(F32)
    for step in range(STEPS):
        lanes = slice(step * chunk, (step + 1) * chunk)
        rows = jnp.concatenate(
            [
                index_ref[:, lanes].astype(F32),
                interp_ref[:, lanes],
                normals_ref[:, lanes],
                jnp.zeros((5, chunk), F32),
            ],
            axis=0,
        )
        columns = rows.T
        mix = jnp.zeros((chunk, nodes), F32)
        for corner in range(4):
            here = columns[:, corner : corner + 1] == node
            mix = mix + jnp.where(here, columns[:, 4 + corner : 5 + corner], 0.0)
        high, low = halves(mix)
        if step == 0:
            copies[3].wait()
        table = jnp.concatenate([modes_ref[0], modes_ref[1], modes_ref[2]], axis=1)
        picked = mm(high, table) + mm(low, table)
        velocity = jnp.zeros((chunk, width), F32)
        for axis_id in range(3):
            part = picked[:, axis_id * width : (axis_id + 1) * width]
            velocity = velocity + columns[:, 8 + axis_id : 9 + axis_id] * part
        blocks = velocity.reshape(chunk // 24, 24, width)
        where = slice(step * chunk // 24, (step + 1) * chunk // 24)
        out_ref[where, 0:16, :] = blocks[:, 0:16, :].astype(BF16)
        out_ref[where, 16:32, :] = blocks[:, 8:24, :].astype(BF16)


def interpolate(node_modes, node_index, interp, normals):
    slots, width = node_index.shape[1], node_modes.shape[2]
    return pl.pallas_call(
        interp_kernel,
        in_specs=[HBM] * 4,
        out_specs=VMEM,
        out_shape=jax.ShapeDtypeStruct((slots // 24, 32, width), BF16),
        scratch_shapes=[
            pltpu.VMEM(node_modes.shape, BF16),
            pltpu.VMEM(node_index.shape, I32),
            pltpu.VMEM(interp.shape, F32),
            pltpu.VMEM(normals.shape, F32),
            pltpu.SemaphoreType.DMA((4,)),
        ],
        compiler_params=WHOLE,
        cost_estimate=pl.CostEstimate(
            flops=2 * slots * 1024 * 384, bytes_accessed=1 << 20, transcendentals=0
        ),
    )(node_modes, node_index, interp, normals)


def prepare_kernel(
    place_ref, rank_ref, count_ref, diag_ref, lower_ref, right_ref, upper_ref, back_ref, area_ref,
    stack_ref, mats_ref, target_ref, scaled_ref, area_out_ref,
):
    panels = diag_ref.shape[0]
    keep = lax.broadcasted_iota(I32, (RANK, panels), 0) < rank_ref[0]
    zero = jnp.zeros((RANK, panels), BF16)
    lower = jnp.where(keep, lower_ref[...], zero)
    upper = jnp.where(keep, upper_ref[...], zero)
    spread = mm_t(diag_ref[...], lower)
    high, low = halves(spread)
    both = jnp.concatenate([right_ref[...], back_ref[...]], axis=0)
    seen = mm(both, jnp.concatenate([high, low], axis=1))
    seen = seen[:, :RANK] + seen[:, RANK:]
    back = mm_t(back_ref[...], upper)
    blank = jnp.zeros((RANK, RANK), F32)
    mats = jnp.concatenate([-seen[:RANK], -back, seen[RANK:], blank], axis=1)
    mats_high, mats_low = halves(mats)
    mats_ref[...] = jnp.concatenate([mats_high, mats_low], axis=0)
    upper_left = upper.astype(F32).T
    stack_ref[...] = jnp.concatenate(
        [high, upper_left.astype(BF16), low, jnp.zeros((panels, RANK), BF16)], axis=1
    )
    area = jnp.broadcast_to(jnp.broadcast_to(area_ref[...], (8, panels)).T[:, 0:1], (panels, 128))
    area_out_ref[...] = area
    gap = jnp.zeros((panels, 3 * RANK), F32)
    minus = -area[:, :RANK]
    scaled_ref[...] = jnp.concatenate(
        [gap, minus * spread, gap, minus * upper_left], axis=1
    ).astype(BF16)
    sources = count_ref.shape[1]
    slots = target_ref.shape[1]
    counts = jnp.broadcast_to(count_ref[...].astype(F32), (16, sources)).astype(BF16)
    source = lax.broadcasted_iota(I32, (sources, slots), 0)
    column = lax.broadcasted_iota(I32, (sources, slots), 1) // SLOT_ROWS
    start = mm(counts, jnp.where(source < column, 1.0, 0.0).astype(BF16))[0:1]
    mine = mm(counts, jnp.where(source == column, 1.0, 0.0).astype(BF16))[0:1]
    slot = lax.broadcasted_iota(I32, (1, slots), 1) % SLOT_ROWS - 4 * place_ref[3]
    slot = slot.astype(F32)
    target_ref[...] = jnp.where((slot >= 0.0) & (slot < mine), start + slot, -1.0)


def prepare(place, rank, count, diag, lower, right, upper, back, area):
    panels, slots = diag.shape[0], count.shape[1] * SLOT_ROWS
    return pl.pallas_call(
        prepare_kernel,
        in_specs=[SMEM, SMEM] + [VMEM] * 7,
        out_specs=[VMEM] * 5,
        out_shape=[
            jax.ShapeDtypeStruct((panels, 4 * RANK), BF16),
            jax.ShapeDtypeStruct((2 * RANK, 4 * RANK), BF16),
            jax.ShapeDtypeStruct((1, slots), F32),
            jax.ShapeDtypeStruct((panels, 8 * RANK), BF16),
            jax.ShapeDtypeStruct((panels, 4 * RANK), F32),
        ],
        compiler_params=PARAMS,
        cost_estimate=pl.CostEstimate(
            flops=4 << 30, bytes_accessed=8 << 20, transcendentals=0
        ),
    )(place, rank, count, diag, lower, right, upper, back, area)


def select_kernel(arrived_ref, target_ref, normal_ref, turned_ref):
    panels, width = normal_ref.shape
    slots = target_ref.shape[1]
    step = 256
    target = target_ref[...]
    arrived = arrived_ref[...]
    parts = []
    for begin in range(0, panels, step):
        panel = (lax.broadcasted_iota(I32, (step, slots), 0) + begin).astype(F32)
        pick = jnp.where(panel == target, 1.0, 0.0).astype(BF16)
        parts.append(mm(pick, arrived).astype(BF16))
    normal = jnp.concatenate(parts, axis=0)
    normal_ref[...] = normal
    row = lax.broadcasted_iota(I32, (width, width), 0)
    mode = (row % 16) // 2 * 16 + row // 16 * 2 + row % 2
    order = jnp.where(lax.broadcasted_iota(I32, (width, width), 1) == mode, 1.0, 0.0)
    turned_ref[...] = mm_t(order.astype(BF16), normal).astype(BF16)


def select(arrived, target, panels):
    width = arrived.shape[1]
    return pl.pallas_call(
        select_kernel,
        in_specs=[VMEM] * 2,
        out_specs=[VMEM] * 2,
        out_shape=[
            jax.ShapeDtypeStruct((panels, width), BF16),
            jax.ShapeDtypeStruct((width, panels), BF16),
        ],
        compiler_params=PARAMS,
        cost_estimate=pl.CostEstimate(
            flops=1 << 29, bytes_accessed=2 << 20, transcendentals=0
        ),
    )(arrived, target)


def solve_kernel(normal_ref, diag_ref, right_ref, back_ref, solved_ref, seen_ref):
    solved = mm(diag_ref[...], normal_ref[...])
    solved_ref[...] = solved
    high, low = halves(solved)
    width = solved.shape[1]
    both = jnp.concatenate([right_ref[...], back_ref[...]], axis=0)
    seen = mm(both, jnp.concatenate([high, low], axis=1))
    seen_ref[...] = (seen[:, :width] + seen[:, width:]).astype(BF16)


def solve(normal, diag, right, back):
    panels, width = normal.shape
    return pl.pallas_call(
        solve_kernel,
        in_specs=[VMEM] * 4,
        out_specs=[VMEM] * 2,
        out_shape=[
            jax.ShapeDtypeStruct((panels, width), F32),
            jax.ShapeDtypeStruct((2 * RANK, width), BF16),
        ],
        compiler_params=PARAMS,
        cost_estimate=pl.CostEstimate(
            flops=1 << 29, bytes_accessed=4 << 20, transcendentals=0
        ),
    )(normal, diag, right, back)


def local_kernel(
    place_ref, solved_ref, scaled_ref, area_ref, turned_ref, other_ref, seen_ref, mats_ref,
    send_ref,
):
    width = solved_ref.shape[1]
    peers = send_ref.shape[0]
    part = width // peers
    weighted = (area_ref[...] * solved_ref[...]).astype(BF16)
    factor = jnp.concatenate([weighted, scaled_ref[...]], axis=1)
    own = mm(turned_ref[...], factor)
    other = mm(other_ref[...], factor)
    even = place_ref[2] == 0
    send_ref[:, 0 : 2 * RANK, :] = jnp.broadcast_to(
        seen_ref[...][None], (peers, 2 * RANK, width)
    )
    mats = mats_ref[...].astype(F32)
    for side in range(2):
        rows = jnp.where(even, other, own) if side else jnp.where(even, own, other)
        high, low = halves(rows[:, :width])
        begin = 4 * RANK + side * part
        send_ref[:, begin : begin + part, :] = high.reshape(peers, part, width)
        begin = begin + RANK
        send_ref[:, begin : begin + part, :] = low.reshape(peers, part, width)
        for which in range(2):
            begin = which * RANK + side * part
            block = rows[:, (1 + which) * width : (2 + which) * width].reshape(peers, part, width)
            block = (block + mats[begin : begin + part][None]).astype(BF16)
            send_ref[:, 2 * RANK + begin : 2 * RANK + begin + part, :] = block


def local(place, solved, scaled, area, turned, other, seen, mats, peers):
    width = solved.shape[1]
    return pl.pallas_call(
        local_kernel,
        in_specs=[SMEM] + [VMEM] * 7,
        out_specs=VMEM,
        out_shape=jax.ShapeDtypeStruct((peers, 6 * RANK, width), BF16),
        compiler_params=PARAMS,
        cost_estimate=pl.CostEstimate(
            flops=1 << 28, bytes_accessed=2 << 20, transcendentals=0
        ),
    )(place, solved, scaled, area, turned, other, seen, mats)


def element(ref, position):
    high = ref[position, 2 * RANK : 3 * RANK, :]
    low = ref[position, 3 * RANK : 4 * RANK, :]

    def wide(which):
        lanes = slice(which * RANK, (which + 1) * RANK)
        return jnp.concatenate([high[:, lanes], low[:, lanes], high[:, lanes]], axis=1)

    vectors = ref[position, 0 : 2 * RANK, :].astype(F32)
    back = high[:, RANK : 2 * RANK].astype(F32) + low[:, RANK : 2 * RANK].astype(F32)
    return vectors[:RANK], vectors[RANK:], [wide(0), wide(2)], back


def gain_step(total, mask, middle):
    factor = total[:, TURN : TURN + RANK]
    if mask is not None:
        factor = factor * mask
    high, low = halves(factor)
    middle_high, middle_low = halves(middle)
    rows = factor.shape[0]
    first = mm(jnp.concatenate([high, low], axis=0), middle_high)
    return total + (first[:rows] + first[rows:] + mm(high, middle_low))


def unit(offset):
    row = lax.broadcasted_iota(I32, (RANK, WIDE), 0)
    lane = lax.broadcasted_iota(I32, (RANK, WIDE), 1)
    return jnp.where(lane == row + offset, 1.0, 0.0).astype(F32)


def inner_kernel(place_ref, got_ref, own_ref, send_ref):
    width = got_ref.shape[2]
    mine = place_ref[0]
    in_t, in_s = TURN, TURN + RANK
    forward = unit(in_s)
    own_s = jnp.zeros_like(forward)
    total = jnp.concatenate([unit(in_t), unit(in_t), jnp.zeros((RANK, WIDE), F32)], axis=0)
    pad = jnp.zeros((RANK, WIDE - width), F32)
    gap, tail = jnp.zeros((RANK, width), F32), jnp.zeros((RANK, WIDE - width - RANK), F32)
    none = jnp.zeros((2 * RANK, WIDE), F32)
    blank = jnp.zeros((RANK, RANK), BF16)
    row = lax.broadcasted_iota(I32, (3 * RANK, RANK), 0)
    middle_rows = (row >= RANK) & (row < 2 * RANK)
    for position in range(got_ref.shape[0]):
        shift, gain, ahead, back = element(got_ref, position)
        by_s = got_ref[position, 2 * RANK : 3 * RANK, 3 * RANK : 4 * RANK]
        by_t = got_ref[position, 3 * RANK : 4 * RANK, 3 * RANK : 4 * RANK].astype(F32)
        fixed = got_ref[position, 4 * RANK : 5 * RANK, :].astype(F32)
        fixed = fixed + got_ref[position, 5 * RANK : 6 * RANK, :].astype(F32)
        ahead = jnp.concatenate(
            ahead + [jnp.concatenate([by_s, blank, by_s], axis=1)], axis=0
        )
        own_s = jnp.where(mine == position, forward, own_s)
        moved = mm(ahead, tall(forward))
        forward = forward + moved[:RANK] + jnp.concatenate([shift, pad], axis=1)
        middle = (
            jnp.concatenate([gain, pad], axis=1)
            + jnp.concatenate([gap, back, tail], axis=1)
            - moved[RANK : 2 * RANK]
        )
        mask = jnp.where(middle_rows & (position <= mine), 0.0, 1.0)
        mass = moved[2 * RANK :] + jnp.concatenate([fixed, by_t, tail], axis=1)
        total = gain_step(total, mask, middle) + jnp.concatenate([none, mass], axis=0)
    own_ref[...] = jnp.concatenate([own_s, total[RANK : 2 * RANK]], axis=0)
    eye = unit(0)[:, :RANK]
    mats = jnp.concatenate(
        [
            forward[:, in_s : in_s + RANK] - eye,
            total[:RANK, in_t : in_t + RANK] - eye,
            -total[:RANK, in_s : in_s + RANK],
            jnp.zeros((RANK, RANK), F32),
        ],
        axis=1,
    )
    high, low = halves(mats)
    message = jnp.concatenate(
        [forward[:, :width].astype(BF16), total[:RANK, :width].astype(BF16), high, low], axis=0
    )
    peers = send_ref.shape[0]
    send_ref[:, 0 : 4 * RANK, :] = jnp.broadcast_to(message[None], (peers, 4 * RANK, width))
    mass = total[2 * RANK :]
    fixed_high, fixed_low = halves(mass[:, :width])
    by_s_high, by_s_low = halves(mass[:, in_s : in_s + RANK])
    by_t_high, by_t_low = halves(mass[:, in_t : in_t + RANK])
    maps = jnp.concatenate([by_s_high, by_s_low, by_t_high, by_t_low], axis=1)
    sources = jnp.concatenate([fixed_high, fixed_low, maps, jnp.zeros_like(maps)], axis=0)
    row = lax.broadcasted_iota(I32, (peers * 16, 4 * RANK), 0)
    column = lax.broadcasted_iota(I32, (peers * 16, 4 * RANK), 1)
    slot = row % 16
    block = jnp.where(slot < 4, slot // 2, jnp.where((slot == 8) | (slot == 9), 2, 3))
    pick = jnp.where(column == block * RANK + row // 16 * 2 + slot % 2, 1.0, 0.0).astype(BF16)
    send_ref[:, 4 * RANK :, :] = mm(pick, sources).astype(BF16).reshape(peers, 16, width)


def inner(place, got, peers):
    return pl.pallas_call(
        inner_kernel,
        in_specs=[SMEM, VMEM],
        out_specs=[VMEM] * 2,
        out_shape=[
            jax.ShapeDtypeStruct((2 * RANK, WIDE), F32),
            jax.ShapeDtypeStruct((peers, 4 * RANK + 16, got.shape[2]), BF16),
        ],
        compiler_params=PARAMS,
    )(place, got)


def outer_kernel(
    place_ref, got_ref, own_ref, solved_ref, stack_ref, potential_ref, mass_ref,
):
    width = got_ref.shape[2]
    mine = place_ref[1]
    forward = jnp.zeros((RANK, width), F32)
    in_s = forward
    total = jnp.concatenate([unit(TURN), jnp.zeros((16, WIDE), F32)], axis=0)
    rest = jnp.zeros((RANK, WIDE - width - RANK), F32)
    none, low_rest = jnp.zeros((RANK, WIDE), F32), jnp.zeros((16, WIDE - width - RANK), F32)
    zero8, zero16 = jnp.zeros((8, 4 * RANK), F32), jnp.zeros((16, RANK), BF16)
    row = lax.broadcasted_iota(I32, (RANK + 16, RANK), 0)
    for position in range(got_ref.shape[0]):
        shift, gain, ahead, back = element(got_ref, position)
        fixed = got_ref[position, 4 * RANK :, :].astype(F32)
        maps = jnp.concatenate([fixed[8:16], zero8], axis=0)
        by_s_high = maps[:, :RANK].astype(BF16)
        by_s_low = maps[:, RANK : 2 * RANK].astype(BF16)
        by_t = maps[:, 2 * RANK : 3 * RANK] + maps[:, 3 * RANK :]
        ahead = jnp.concatenate(
            ahead + [jnp.concatenate([by_s_high, by_s_low, by_s_high], axis=1)], axis=0
        )
        in_s = jnp.where(mine == position, forward, in_s)
        moved = mm(ahead, tall(forward))
        forward = forward + moved[:RANK] + shift
        middle = jnp.concatenate([gain - moved[RANK : 2 * RANK], back, rest], axis=1)
        mask = jnp.where((row < RANK) & (position <= mine), 0.0, 1.0)
        mass = jnp.concatenate([fixed + moved[2 * RANK :], by_t, low_rest], axis=1)
        total = gain_step(total, mask, middle) + jnp.concatenate([none, mass], axis=0)
    in_t = total[:RANK, :width]
    mass = total[RANK:, :width]
    mass_ref[...] = mass[0:2] + mass[2:4]
    own = own_ref[...]
    map_high, map_low = halves(own[:, width : width + 2 * RANK])
    maps = jnp.concatenate([map_high, map_low, map_high], axis=1)
    state = own[:, :width] + mm(maps, tall(jnp.concatenate([in_t, in_s], axis=0)))
    high, low = halves(state)
    blank = jnp.zeros((RANK, width), BF16)
    left = jnp.concatenate([high, high[:RANK], blank], axis=0)
    right = jnp.concatenate([low, blank, blank], axis=0)
    fixed = mm(stack_ref[...], jnp.concatenate([left, right], axis=1))
    potential = solved_ref[...] - (fixed[:, :width] + fixed[:, width:])
    potential_ref[...] = potential.astype(BF16)


def outer(place, got, own, solved, stack):
    panels, width = solved.shape
    return pl.pallas_call(
        outer_kernel,
        in_specs=[SMEM] + [VMEM] * 4,
        out_specs=[VMEM] * 2,
        out_shape=[
            jax.ShapeDtypeStruct((panels, width), BF16),
            jax.ShapeDtypeStruct((2, width), F32),
        ],
        compiler_params=PARAMS,
    )(place, got, own, solved, stack)


def body(
    node_modes, node_index, interp, normals, counts, inverse_diag,
    lower_left, lower_right, upper_left, upper_right, ranks, areas,
):
    devices, width = lax.axis_size(AXES), node_modes.shape[2]
    inner_size, outer_size = lax.axis_size("z"), lax.axis_size(("y", "x"))
    depth, group = lax.axis_index("z"), lax.axis_index(("y", "x"))
    place = jnp.stack([depth, group, lax.axis_index("side"), depth % 2]).astype(I32)
    outgoing = interpolate(node_modes, node_index, interp, normals)
    arrived = lax.all_to_all(
        outgoing.reshape(devices, SLOT_ROWS, width), AXES, split_axis=0, concat_axis=0, tiled=True
    ).reshape(devices * SLOT_ROWS, width)
    right, back = lower_right.T, upper_right.T
    stack, mats, target, scaled, area = prepare(
        place, ranks, counts.reshape(1, devices), inverse_diag, lower_left.T, right,
        upper_left.T, back, areas.reshape(1, -1),
    )
    normal, turned = select(arrived, target, inverse_diag.shape[0])
    other = lax.ppermute(turned, "side", [(0, 1), (1, 0)])
    solved, seen = solve(normal, inverse_diag, right, back)
    send = local(place, solved, scaled, area, turned, other, seen, mats, inner_size)
    got = lax.all_to_all(send, "z", split_axis=0, concat_axis=0, tiled=True)
    own, send = inner(place, got, outer_size)
    got = lax.all_to_all(send, ("y", "x"), split_axis=0, concat_axis=0, tiled=True)
    return outer(place, got, own, solved, stack)


def solution(mesh):
    grid = jax.sharding.Mesh(mesh.devices.reshape(2, 4, 4, 8), ("side",) + AXES)
    in_specs = (
        P(None, AXES, "side"),
        P(None, AXES),
        P(None, AXES),
        P(None, AXES),
        P(None, AXES),
        P(AXES, None),
        P(AXES, None),
        P(AXES, None),
        P(AXES, None),
        P(AXES, None),
        P(AXES),
        P(AXES),
    )
    out_specs = (P(AXES, "side"), P(AXES, "side"))
    return jax.shard_map(body, mesh=grid, in_specs=in_specs, out_specs=out_specs, check_vma=False)
```

```python
import functools
import jax
import jax.numpy as jnp
from jax import lax
from jax.experimental import pallas as pl
from jax.experimental.pallas import tpu as pltpu
from jax.sharding import PartitionSpec as P

F32, BF16, I32 = jnp.float32, jnp.bfloat16, jnp.int32
AXES = ("y", "x", "z")
RANK, CAP, SLOT_ROWS, WIDE = 32, 12, 16, 256
PARAMS = pltpu.CompilerParams(vmem_limit_bytes=28 * 1024 * 1024)
WHOLE = pltpu.CompilerParams(vmem_limit_bytes=62 * 1024 * 1024)
VMEM = pl.BlockSpec(memory_space=pltpu.VMEM)
SMEM = pl.BlockSpec(memory_space=pltpu.SMEM)
HBM = pl.BlockSpec(memory_space=pltpu.HBM)
STEPS, TURN, GROUPS = 4, 128, 4


def mm(a, b):
    return lax.dot_general(a, b, (((1,), (0,)), ((), ())), preferred_element_type=F32)


def mm_t(a, b):
    return lax.dot_general(a, b, (((1,), (1,)), ((), ())), preferred_element_type=F32)


def halves(value):
    high = value.astype(BF16)
    return high, (value - high.astype(F32)).astype(BF16)


def tall(value):
    high, low = halves(value)
    return jnp.concatenate([high, high, low], axis=0)


def interp_kernel(
    modes_hbm, index_hbm, interp_hbm, normals_hbm, out_ref,
    modes_ref, index_ref, interp_ref, normals_ref, sems,
):
    pairs = [
        (index_hbm, index_ref), (interp_hbm, interp_ref), (normals_hbm, normals_ref),
        (modes_hbm, modes_ref),
    ]
    copies = [
        pltpu.make_async_copy(source, target, sems.at[number])
        for number, (source, target) in enumerate(pairs)
    ]
    for copy in copies:
        copy.start()
    for copy in copies[:3]:
        copy.wait()
    slots, nodes = index_ref.shape[1], modes_ref.shape[1]
    width = modes_ref.shape[2]
    chunk = slots // STEPS
    node = lax.broadcasted_iota(I32, (chunk, nodes), 1).astype(F32)
    for step in range(STEPS):
        lanes = slice(step * chunk, (step + 1) * chunk)
        rows = jnp.concatenate(
            [
                index_ref[:, lanes].astype(F32),
                interp_ref[:, lanes],
                normals_ref[:, lanes],
                jnp.zeros((5, chunk), F32),
            ],
            axis=0,
        )
        columns = rows.T
        mix = jnp.zeros((chunk, nodes), F32)
        for corner in range(4):
            here = columns[:, corner : corner + 1] == node
            mix = mix + jnp.where(here, columns[:, 4 + corner : 5 + corner], 0.0)
        high, low = halves(mix)
        if step == 0:
            copies[3].wait()
        table = jnp.concatenate([modes_ref[0], modes_ref[1], modes_ref[2]], axis=1)
        picked = mm(high, table) + mm(low, table)
        velocity = jnp.zeros((chunk, width), F32)
        for axis_id in range(3):
            part = picked[:, axis_id * width : (axis_id + 1) * width]
            velocity = velocity + columns[:, 8 + axis_id : 9 + axis_id] * part
        blocks = velocity.reshape(chunk // 24, 24, width)
        where = slice(step * chunk // 24, (step + 1) * chunk // 24)
        out_ref[where, 0:16, :] = blocks[:, 0:16, :].astype(BF16)
        out_ref[where, 16:32, :] = blocks[:, 8:24, :].astype(BF16)


def interpolate(node_modes, node_index, interp, normals):
    slots, width = node_index.shape[1], node_modes.shape[2]
    return pl.pallas_call(
        interp_kernel,
        in_specs=[HBM] * 4,
        out_specs=VMEM,
        out_shape=jax.ShapeDtypeStruct((slots // 24, 32, width), BF16),
        scratch_shapes=[
            pltpu.VMEM(node_modes.shape, BF16),
            pltpu.VMEM(node_index.shape, I32),
            pltpu.VMEM(interp.shape, F32),
            pltpu.VMEM(normals.shape, F32),
            pltpu.SemaphoreType.DMA((4,)),
        ],
        compiler_params=WHOLE,
        cost_estimate=pl.CostEstimate(
            flops=2 * slots * 1024 * 384, bytes_accessed=1 << 20, transcendentals=0
        ),
    )(node_modes, node_index, interp, normals)


def prepare_kernel(
    place_ref, rank_ref, count_ref, diag_ref, lower_ref, right_ref, upper_ref, back_ref, area_ref,
    stack_ref, mats_ref, target_ref, scaled_ref, area_out_ref,
):
    panels = diag_ref.shape[0]
    keep = lax.broadcasted_iota(I32, (RANK, panels), 0) < rank_ref[0]
    zero = jnp.zeros((RANK, panels), BF16)
    lower = jnp.where(keep, lower_ref[...], zero)
    upper = jnp.where(keep, upper_ref[...], zero)
    spread = mm_t(diag_ref[...], lower)
    high, low = halves(spread)
    both = jnp.concatenate([right_ref[...], back_ref[...]], axis=0)
    seen = mm(both, jnp.concatenate([high, low], axis=1))
    seen = seen[:, :RANK] + seen[:, RANK:]
    back = mm_t(back_ref[...], upper)
    blank = jnp.zeros((RANK, RANK), F32)
    mats = jnp.concatenate([-seen[:RANK], -back, seen[RANK:], blank], axis=1)
    mats_high, mats_low = halves(mats)
    mats_ref[...] = jnp.concatenate([mats_high, mats_low], axis=0)
    upper_left = upper.astype(F32).T
    stack_ref[...] = jnp.concatenate(
        [high, upper_left.astype(BF16), low, jnp.zeros((panels, RANK), BF16)], axis=1
    )
    area = jnp.broadcast_to(jnp.broadcast_to(area_ref[...], (8, panels)).T[:, 0:1], (panels, 128))
    area_out_ref[...] = area
    gap = jnp.zeros((panels, 3 * RANK), F32)
    minus = -area[:, :RANK]
    scaled_ref[...] = jnp.concatenate(
        [gap, minus * spread, gap, minus * upper_left], axis=1
    ).astype(BF16)
    sources = count_ref.shape[1]
    slots = target_ref.shape[1]
    counts = jnp.broadcast_to(count_ref[...].astype(F32), (16, sources)).astype(BF16)
    source = lax.broadcasted_iota(I32, (sources, slots), 0)
    column = lax.broadcasted_iota(I32, (sources, slots), 1) // SLOT_ROWS
    start = mm(counts, jnp.where(source < column, 1.0, 0.0).astype(BF16))[0:1]
    mine = mm(counts, jnp.where(source == column, 1.0, 0.0).astype(BF16))[0:1]
    slot = lax.broadcasted_iota(I32, (1, slots), 1) % SLOT_ROWS - 4 * place_ref[3]
    slot = slot.astype(F32)
    target_ref[...] = jnp.where((slot >= 0.0) & (slot < mine), start + slot, -1.0)


def prepare(place, rank, count, diag, lower, right, upper, back, area):
    panels, slots = diag.shape[0], count.shape[1] * SLOT_ROWS
    return pl.pallas_call(
        prepare_kernel,
        in_specs=[SMEM, SMEM] + [VMEM] * 7,
        out_specs=[VMEM] * 5,
        out_shape=[
            jax.ShapeDtypeStruct((panels, 4 * RANK), BF16),
            jax.ShapeDtypeStruct((2 * RANK, 4 * RANK), BF16),
            jax.ShapeDtypeStruct((1, slots), F32),
            jax.ShapeDtypeStruct((panels, 8 * RANK), BF16),
            jax.ShapeDtypeStruct((panels, 4 * RANK), F32),
        ],
        compiler_params=PARAMS,
        cost_estimate=pl.CostEstimate(
            flops=4 << 30, bytes_accessed=8 << 20, transcendentals=0
        ),
    )(place, rank, count, diag, lower, right, upper, back, area)


def select_kernel(arrived_ref, target_ref, normal_ref, turned_ref):
    panels, width = normal_ref.shape
    target = target_ref[...]
    sources = target.shape[1] // SLOT_ROWS
    step = 256
    parts = []
    for begin in range(0, panels, step):
        least = max(0, (begin - CAP + 1) // CAP)
        most = min(sources, (begin + step - 1 + CAP * sources - panels) // CAP + 1)
        first = least * SLOT_ROWS // 128 * 128
        last = -(-most * SLOT_ROWS // 128) * 128
        panel = (lax.broadcasted_iota(I32, (step, last - first), 0) + begin).astype(F32)
        pick = jnp.where(panel == target[:, first:last], 1.0, 0.0).astype(BF16)
        parts.append(mm(pick, arrived_ref[first:last, :]).astype(BF16))
    normal = jnp.concatenate(parts, axis=0)
    normal_ref[...] = normal
    row = lax.broadcasted_iota(I32, (width, width), 0)
    mode = (row % 16) // 2 * 16 + row // 16 * 2 + row % 2
    order = jnp.where(lax.broadcasted_iota(I32, (width, width), 1) == mode, 1.0, 0.0)
    turned_ref[...] = mm_t(order.astype(BF16), normal).astype(BF16)


def select(arrived, target, panels):
    width = arrived.shape[1]
    return pl.pallas_call(
        select_kernel,
        in_specs=[VMEM] * 2,
        out_specs=[VMEM] * 2,
        out_shape=[
            jax.ShapeDtypeStruct((panels, width), BF16),
            jax.ShapeDtypeStruct((width, panels), BF16),
        ],
        compiler_params=PARAMS,
        cost_estimate=pl.CostEstimate(
            flops=1 << 29, bytes_accessed=2 << 20, transcendentals=0
        ),
    )(arrived, target)


def solve_kernel(normal_ref, diag_ref, right_ref, back_ref, solved_ref, seen_ref):
    solved = mm(diag_ref[...], normal_ref[...])
    solved_ref[...] = solved
    high, low = halves(solved)
    width = solved.shape[1]
    both = jnp.concatenate([right_ref[...], back_ref[...]], axis=0)
    seen = mm(both, jnp.concatenate([high, low], axis=1))
    seen_ref[...] = (seen[:, :width] + seen[:, width:]).astype(BF16)


def solve(normal, diag, right, back):
    panels, width = normal.shape
    return pl.pallas_call(
        solve_kernel,
        in_specs=[VMEM] * 4,
        out_specs=[VMEM] * 2,
        out_shape=[
            jax.ShapeDtypeStruct((panels, width), F32),
            jax.ShapeDtypeStruct((2 * RANK, width), BF16),
        ],
        compiler_params=PARAMS,
        cost_estimate=pl.CostEstimate(
            flops=1 << 29, bytes_accessed=4 << 20, transcendentals=0
        ),
    )(normal, diag, right, back)


def local_kernel(
    place_ref, solved_ref, scaled_ref, area_ref, turned_ref, other_ref, seen_ref, mats_ref,
    send_ref,
):
    width = solved_ref.shape[1]
    peers = send_ref.shape[0]
    part = width // peers
    weighted = (area_ref[...] * solved_ref[...]).astype(BF16)
    factor = jnp.concatenate([weighted, scaled_ref[...]], axis=1)
    own = mm(turned_ref[...], factor)
    other = mm(other_ref[...], factor)
    even = place_ref[2] == 0
    send_ref[:, 0 : 2 * RANK, :] = jnp.broadcast_to(
        seen_ref[...][None], (peers, 2 * RANK, width)
    )
    mats = mats_ref[...].astype(F32)
    for side in range(2):
        rows = jnp.where(even, other, own) if side else jnp.where(even, own, other)
        begin = 4 * RANK + side * part
        fixed = rows[:, :width].astype(BF16)
        send_ref[:, begin : begin + part, :] = fixed.reshape(peers, part, width)
        for which in range(2):
            begin = which * RANK + side * part
            block = rows[:, (1 + which) * width : (2 + which) * width].reshape(peers, part, width)
            block = (block + mats[begin : begin + part][None]).astype(BF16)
            send_ref[:, 2 * RANK + begin : 2 * RANK + begin + part, :] = block


def local(place, solved, scaled, area, turned, other, seen, mats, peers):
    width = solved.shape[1]
    return pl.pallas_call(
        local_kernel,
        in_specs=[SMEM] + [VMEM] * 7,
        out_specs=VMEM,
        out_shape=jax.ShapeDtypeStruct((peers, 5 * RANK, width), BF16),
        compiler_params=PARAMS,
        cost_estimate=pl.CostEstimate(
            flops=1 << 28, bytes_accessed=2 << 20, transcendentals=0
        ),
    )(place, solved, scaled, area, turned, other, seen, mats)


def element(ref, position):
    high = ref[position, 2 * RANK : 3 * RANK, :]
    low = ref[position, 3 * RANK : 4 * RANK, :]

    def wide(which):
        lanes = slice(which * RANK, (which + 1) * RANK)
        return jnp.concatenate([high[:, lanes], low[:, lanes], high[:, lanes]], axis=1)

    vectors = ref[position, 0 : 2 * RANK, :].astype(F32)
    back = high[:, RANK : 2 * RANK].astype(F32) + low[:, RANK : 2 * RANK].astype(F32)
    return vectors[:RANK], vectors[RANK:], [wide(0), wide(2)], back


def gain_step(total, mask, middle):
    factor = total[:, TURN : TURN + RANK]
    if mask is not None:
        factor = factor * mask
    high, low = halves(factor)
    middle_high, middle_low = halves(middle)
    rows = factor.shape[0]
    first = mm(jnp.concatenate([high, low], axis=0), middle_high)
    return total + (first[:rows] + first[rows:] + mm(high, middle_low))


def unit(offset):
    row = lax.broadcasted_iota(I32, (RANK, WIDE), 0)
    lane = lax.broadcasted_iota(I32, (RANK, WIDE), 1)
    return jnp.where(lane == row + offset, 1.0, 0.0).astype(F32)


def advance(forward, total, parts, mask):
    shift, gain, ahead, back, by_s, by_t, fixed = parts
    width = fixed.shape[1]
    pad = jnp.zeros((RANK, WIDE - width), F32)
    gap, tail = jnp.zeros((RANK, width), F32), jnp.zeros((RANK, WIDE - width - RANK), F32)
    moved = mm(jnp.concatenate(ahead + [by_s], axis=0), tall(forward))
    later = forward + moved[:RANK] + jnp.concatenate([shift, pad], axis=1)
    middle = (
        jnp.concatenate([gain, pad], axis=1)
        + jnp.concatenate([gap, back, tail], axis=1)
        - moved[RANK : 2 * RANK]
    )
    mass = moved[2 * RANK :] + jnp.concatenate([fixed, by_t, tail[: fixed.shape[0]]], axis=1)
    none = jnp.zeros((2 * RANK, WIDE), F32)
    total = gain_step(total, mask, middle) + jnp.concatenate([none, mass], axis=0)
    return later, total


def own_mask(rows, keep):
    row = lax.broadcasted_iota(I32, (rows, RANK), 0)
    return jnp.where((row >= RANK) & (row < 2 * RANK) & jnp.logical_not(keep), 0.0, 1.0)


def start_total(rows):
    head = [unit(TURN), unit(TURN)]
    return jnp.concatenate(head + [jnp.zeros((rows, WIDE), F32)], axis=0)


def inner_kernel(place_ref, got_ref, own_ref, send_ref):
    width = got_ref.shape[2]
    mine = place_ref[0]
    in_t, in_s = TURN, TURN + RANK
    forward, total = unit(in_s), start_total(RANK)
    own_s = jnp.zeros_like(forward)
    blank = jnp.zeros((RANK, RANK), BF16)
    for position in range(got_ref.shape[0]):
        by_s = got_ref[position, 2 * RANK : 3 * RANK, 3 * RANK : 4 * RANK]
        by_t = got_ref[position, 3 * RANK : 4 * RANK, 3 * RANK : 4 * RANK].astype(F32)
        fixed = got_ref[position, 4 * RANK : 5 * RANK, :].astype(F32)
        by_s = jnp.concatenate([by_s, blank, by_s], axis=1)
        own_s = jnp.where(mine == position, forward, own_s)
        forward, total = advance(
            forward, total, element(got_ref, position) + (by_s, by_t, fixed),
            own_mask(3 * RANK, position > mine),
        )
    own_ref[...] = jnp.concatenate([own_s, total[RANK : 2 * RANK]], axis=0)
    eye = unit(0)[:, :RANK]
    mats = jnp.concatenate(
        [
            forward[:, in_s : in_s + RANK] - eye,
            total[:RANK, in_t : in_t + RANK] - eye,
            -total[:RANK, in_s : in_s + RANK],
            jnp.zeros((RANK, RANK), F32),
        ],
        axis=1,
    )
    high, low = halves(mats)
    message = jnp.concatenate(
        [forward[:, :width].astype(BF16), total[:RANK, :width].astype(BF16), high, low], axis=0
    )
    peers = send_ref.shape[0]
    send_ref[:, 0 : 4 * RANK, :] = jnp.broadcast_to(message[None], (peers, 4 * RANK, width))
    mass = total[2 * RANK :]
    fixed_high, fixed_low = halves(mass[:, :width])
    by_s_high, by_s_low = halves(mass[:, in_s : in_s + RANK])
    by_t_high, by_t_low = halves(mass[:, in_t : in_t + RANK])
    maps = jnp.concatenate([by_s_high, by_s_low, by_t_high, by_t_low], axis=1)
    sources = jnp.concatenate([fixed_high, fixed_low, maps, jnp.zeros_like(maps)], axis=0)
    row = lax.broadcasted_iota(I32, (peers * 16, 4 * RANK), 0)
    column = lax.broadcasted_iota(I32, (peers * 16, 4 * RANK), 1)
    slot = row % 16
    block = jnp.where(slot < 4, slot // 2, jnp.where((slot == 8) | (slot == 9), 2, 3))
    pick = jnp.where(column == block * RANK + row // 16 * 2 + slot % 2, 1.0, 0.0).astype(BF16)
    send_ref[:, 4 * RANK :, :] = mm(pick, sources).astype(BF16).reshape(peers, 16, width)


def inner(place, got, peers):
    return pl.pallas_call(
        inner_kernel,
        in_specs=[SMEM, VMEM],
        out_specs=[VMEM] * 2,
        out_shape=[
            jax.ShapeDtypeStruct((2 * RANK, WIDE), F32),
            jax.ShapeDtypeStruct((peers, 4 * RANK + 16, got.shape[2]), BF16),
        ],
        compiler_params=PARAMS,
    )(place, got)


def outer_kernel(
    place_ref, got_ref, own_ref, solved_ref, stack_ref, potential_ref, mass_ref,
):
    width = got_ref.shape[2]
    groups = GROUPS
    members = got_ref.shape[0] // groups
    my_group, my_member = place_ref[1] // members, place_ref[1] % members
    in_t, in_s = TURN, TURN + RANK
    forwards = [unit(in_s)] * groups
    totals = [start_total(16)] * groups
    own_s = jnp.zeros((RANK, WIDE), F32)
    zero8 = jnp.zeros((8, 4 * RANK), F32)
    for member in range(members):
        mask = own_mask(2 * RANK + 16, member > my_member)
        for group in range(groups):
            position = group * members + member
            fixed = got_ref[position, 4 * RANK :, :].astype(F32)
            maps = jnp.concatenate([fixed[8:16], zero8], axis=0)
            by_s = maps[:, :RANK].astype(BF16)
            by_s = jnp.concatenate(
                [by_s, maps[:, RANK : 2 * RANK].astype(BF16), by_s], axis=1
            )
            by_t = maps[:, 2 * RANK : 3 * RANK] + maps[:, 3 * RANK :]
            here = (my_group == group) & (my_member == member)
            own_s = jnp.where(here, forwards[group], own_s)
            forwards[group], totals[group] = advance(
                forwards[group], totals[group],
                element(got_ref, position) + (by_s, by_t, fixed), mask,
            )
    own_t = jnp.zeros((RANK, WIDE), F32)
    for group in range(groups):
        own_t = jnp.where(my_group == group, totals[group][RANK : 2 * RANK], own_t)
    own = own_ref[...]
    map_high, map_low = halves(own[:, width : width + 2 * RANK])
    maps = jnp.concatenate([map_high, map_low, map_high], axis=1)
    lanes = lax.broadcasted_iota(I32, own.shape, 1)
    own = jnp.where(lanes < width, own, 0.0) + mm(
        maps, tall(jnp.concatenate([own_t, own_s], axis=0))
    )
    eye = unit(0)[:, :RANK]
    forward = jnp.zeros((RANK, width), F32)
    enter_s = forward
    total = jnp.concatenate([unit(TURN), jnp.zeros((16, WIDE), F32)], axis=0)
    none, rest = jnp.zeros((RANK, WIDE), F32), jnp.zeros((RANK, WIDE - width - RANK), F32)
    row = lax.broadcasted_iota(I32, (RANK + 16, RANK), 0)
    for group in range(groups):
        step, whole = forwards[group], totals[group]
        mass = whole[2 * RANK :]
        ahead = jnp.concatenate(
            [
                step[:, in_s : in_s + RANK] - eye,
                whole[:RANK, in_s : in_s + RANK],
                mass[:, in_s : in_s + RANK],
            ],
            axis=0,
        )
        high, low = halves(ahead)
        enter_s = jnp.where(my_group == group, forward, enter_s)
        moved = mm(jnp.concatenate([high, low, high], axis=1), tall(forward))
        forward = forward + moved[:RANK] + step[:, :width]
        middle = jnp.concatenate(
            [
                whole[:RANK, :width] + moved[RANK : 2 * RANK],
                whole[:RANK, in_t : in_t + RANK] - eye,
                rest,
            ],
            axis=1,
        )
        mask = jnp.where((row < RANK) & (group <= my_group), 0.0, 1.0)
        mass = jnp.concatenate(
            [mass[:, :width] + moved[2 * RANK :], mass[:, in_t : in_t + RANK], rest[:16]], axis=1
        )
        total = gain_step(total, mask, middle) + jnp.concatenate([none, mass], axis=0)
    enter_t = total[:RANK, :width]
    mass = total[RANK:, :width]
    mass_ref[...] = mass[0:2] + mass[2:4]
    map_high, map_low = halves(own[:, width : width + 2 * RANK])
    maps = jnp.concatenate([map_high, map_low, map_high], axis=1)
    state = own[:, :width] + mm(maps, tall(jnp.concatenate([enter_t, enter_s], axis=0)))
    high, low = halves(state)
    blank = jnp.zeros((RANK, width), BF16)
    left = jnp.concatenate([high, high[:RANK], blank], axis=0)
    right = jnp.concatenate([low, blank, blank], axis=0)
    fixed = mm(stack_ref[...], jnp.concatenate([left, right], axis=1))
    potential = solved_ref[...] - (fixed[:, :width] + fixed[:, width:])
    potential_ref[...] = potential.astype(BF16)


def outer(place, got, own, solved, stack):
    panels, width = solved.shape
    return pl.pallas_call(
        outer_kernel,
        in_specs=[SMEM] + [VMEM] * 4,
        out_specs=[VMEM] * 2,
        out_shape=[
            jax.ShapeDtypeStruct((panels, width), BF16),
            jax.ShapeDtypeStruct((2, width), F32),
        ],
        compiler_params=PARAMS,
    )(place, got, own, solved, stack)


def body(
    node_modes, node_index, interp, normals, counts, inverse_diag,
    lower_left, lower_right, upper_left, upper_right, ranks, areas,
):
    devices, width = lax.axis_size(AXES), node_modes.shape[2]
    inner_size, outer_size = lax.axis_size("z"), lax.axis_size(("y", "x"))
    depth, group = lax.axis_index("z"), lax.axis_index(("y", "x"))
    place = jnp.stack([depth, group, lax.axis_index("side"), depth % 2]).astype(I32)
    outgoing = interpolate(node_modes, node_index, interp, normals)
    arrived = lax.all_to_all(
        outgoing.reshape(devices, SLOT_ROWS, width), AXES, split_axis=0, concat_axis=0, tiled=True
    ).reshape(devices * SLOT_ROWS, width)
    right, back = lower_right.T, upper_right.T
    stack, mats, target, scaled, area = prepare(
        place, ranks, counts.reshape(1, devices), inverse_diag, lower_left.T, right,
        upper_left.T, back, areas.reshape(1, -1),
    )
    normal, turned = select(arrived, target, inverse_diag.shape[0])
    other = lax.ppermute(turned, "side", [(0, 1), (1, 0)])
    solved, seen = solve(normal, inverse_diag, right, back)
    send = local(place, solved, scaled, area, turned, other, seen, mats, inner_size)
    got = lax.all_to_all(send, "z", split_axis=0, concat_axis=0, tiled=True)
    own, send = inner(place, got, outer_size)
    got = lax.all_to_all(send, ("y", "x"), split_axis=0, concat_axis=0, tiled=True)
    return outer(place, got, own, solved, stack)


def solution(mesh):
    grid = jax.sharding.Mesh(mesh.devices.reshape(2, 4, 4, 8), ("side",) + AXES)
    in_specs = (
        P(None, AXES, "side"),
        P(None, AXES),
        P(None, AXES),
        P(None, AXES),
        P(None, AXES),
        P(AXES, None),
        P(AXES, None),
        P(AXES, None),
        P(AXES, None),
        P(AXES, None),
        P(AXES),
        P(AXES),
    )
    out_specs = (P(AXES, "side"), P(AXES, "side"))
    return jax.shard_map(body, mesh=grid, in_specs=in_specs, out_specs=out_specs, check_vma=False)
```

```python
import functools
import jax
import jax.numpy as jnp
from jax import lax
from jax.experimental import pallas as pl
from jax.experimental.pallas import tpu as pltpu
from jax.sharding import PartitionSpec as P

F32, BF16, I32 = jnp.float32, jnp.bfloat16, jnp.int32
AXES = ("y", "x", "z")
RANK, CAP, SLOT_ROWS, WIDE = 32, 12, 16, 256
PARAMS = pltpu.CompilerParams(vmem_limit_bytes=28 * 1024 * 1024)
WHOLE = pltpu.CompilerParams(vmem_limit_bytes=62 * 1024 * 1024)
VMEM = pl.BlockSpec(memory_space=pltpu.VMEM)
SMEM = pl.BlockSpec(memory_space=pltpu.SMEM)
HBM = pl.BlockSpec(memory_space=pltpu.HBM)
STEPS, TURN, GROUPS = 4, 128, 2
TILE, LANES, ROWS = 32, 256, 192


def mm(a, b):
    return lax.dot_general(a, b, (((1,), (0,)), ((), ())), preferred_element_type=F32)


def mm_t(a, b):
    return lax.dot_general(a, b, (((1,), (1,)), ((), ())), preferred_element_type=F32)


def halves(value):
    high = value.astype(BF16)
    return high, (value - high.astype(F32)).astype(BF16)


def tall(value):
    high, low = halves(value)
    return jnp.concatenate([high, high, low], axis=0)


def interp_kernel(
    modes_hbm, index_hbm, interp_hbm, normals_hbm, out_hbm,
    modes_ref, index_ref, interp_ref, normals_ref, high_ref, low_ref, out_ref, sems, out_sems,
):
    pairs = [
        (index_hbm, index_ref), (interp_hbm, interp_ref), (normals_hbm, normals_ref),
        (modes_hbm, modes_ref),
    ]
    copies = [
        pltpu.make_async_copy(source, target, sems.at[number])
        for number, (source, target) in enumerate(pairs)
    ]
    for copy in copies:
        copy.start()
    for copy in copies[:3]:
        copy.wait()
    slots, nodes = index_ref.shape[1], modes_ref.shape[1]
    width = modes_ref.shape[2]
    chunk = slots // STEPS
    node = lax.broadcasted_iota(I32, (TILE, nodes), 1).astype(F32)
    leaving = []
    for step in range(STEPS):
        lanes = slice(step * chunk, (step + 1) * chunk)
        rows = jnp.concatenate(
            [
                index_ref[:, lanes].astype(F32),
                interp_ref[:, lanes],
                normals_ref[:, lanes],
                jnp.zeros((5, chunk), F32),
            ],
            axis=0,
        )
        columns = rows.T
        if step == 0:
            copies[3].wait()
        for begin in range(0, chunk, TILE):
            part = columns[begin : begin + TILE]
            for lane in range(0, nodes, LANES):
                mix = jnp.zeros((TILE, LANES), F32)
                for corner in range(4):
                    here = part[:, corner : corner + 1] == node[:, lane : lane + LANES]
                    mix = mix + jnp.where(here, part[:, 4 + corner : 5 + corner], 0.0)
                high, low = halves(mix)
                high_ref[step % 2, begin : begin + TILE, lane : lane + LANES] = high
                low_ref[step % 2, begin : begin + TILE, lane : lane + LANES] = low
        table = jnp.concatenate([modes_ref[0], modes_ref[1], modes_ref[2]], axis=1)
        for begin in range(0, chunk, ROWS):
            picked = mm(high_ref[step % 2, begin : begin + ROWS], table) + mm(
                low_ref[step % 2, begin : begin + ROWS], table
            )
            velocity = jnp.zeros((ROWS, width), F32)
            for axis_id in range(3):
                part = picked[:, axis_id * width : (axis_id + 1) * width]
                normal = columns[begin : begin + ROWS, 8 + axis_id : 9 + axis_id]
                velocity = velocity + normal * part
            blocks = velocity.reshape(ROWS // 24, 24, width)
            where = slice((step * chunk + begin) // 24, (step * chunk + begin + ROWS) // 24)
            out_ref[where, 0:16, :] = blocks[:, 0:16, :].astype(BF16)
            out_ref[where, 16:32, :] = blocks[:, 8:24, :].astype(BF16)
        where = pl.ds(step * chunk // 24, chunk // 24)
        leaving.append(
            pltpu.make_async_copy(out_ref.at[where], out_hbm.at[where], out_sems.at[step])
        )
        leaving[-1].start()
    for copy in leaving:
        copy.wait()


def interpolate(node_modes, node_index, interp, normals):
    slots, width = node_index.shape[1], node_modes.shape[2]
    return pl.pallas_call(
        interp_kernel,
        in_specs=[HBM] * 4,
        out_specs=HBM,
        out_shape=jax.ShapeDtypeStruct((slots // 24, 32, width), BF16),
        scratch_shapes=[
            pltpu.VMEM(node_modes.shape, BF16),
            pltpu.VMEM(node_index.shape, I32),
            pltpu.VMEM(interp.shape, F32),
            pltpu.VMEM(normals.shape, F32),
            pltpu.VMEM((2, slots // STEPS, node_modes.shape[1]), BF16),
            pltpu.VMEM((2, slots // STEPS, node_modes.shape[1]), BF16),
            pltpu.VMEM((slots // 24, 32, width), BF16),
            pltpu.SemaphoreType.DMA((4,)),
            pltpu.SemaphoreType.DMA((STEPS,)),
        ],
        compiler_params=WHOLE,
        cost_estimate=pl.CostEstimate(
            flops=2 * slots * 1024 * 384, bytes_accessed=1 << 20, transcendentals=0
        ),
    )(node_modes, node_index, interp, normals)


def prepare_kernel(
    place_ref, rank_ref, count_ref, diag_ref, lower_ref, right_ref, upper_ref, back_ref, area_ref,
    stack_ref, mats_ref, target_ref, scaled_ref, area_out_ref,
):
    panels = diag_ref.shape[0]
    keep = lax.broadcasted_iota(I32, (RANK, panels), 0) < rank_ref[0]
    zero = jnp.zeros((RANK, panels), BF16)
    lower = jnp.where(keep, lower_ref[...], zero)
    upper = jnp.where(keep, upper_ref[...], zero)
    spread = mm_t(diag_ref[...], lower)
    high, low = halves(spread)
    both = jnp.concatenate([right_ref[...], back_ref[...]], axis=0)
    seen = mm(both, jnp.concatenate([high, low], axis=1))
    seen = seen[:, :RANK] + seen[:, RANK:]
    back = mm_t(back_ref[...], upper)
    blank = jnp.zeros((RANK, RANK), F32)
    mats = jnp.concatenate([-seen[:RANK], -back, seen[RANK:], blank], axis=1)
    mats_high, mats_low = halves(mats)
    mats_ref[...] = jnp.concatenate([mats_high, mats_low], axis=0)
    upper_left = upper.astype(F32).T
    stack_ref[...] = jnp.concatenate(
        [high, upper_left.astype(BF16), low, jnp.zeros((panels, RANK), BF16)], axis=1
    )
    area = jnp.broadcast_to(jnp.broadcast_to(area_ref[...], (8, panels)).T[:, 0:1], (panels, 128))
    area_out_ref[...] = area
    gap = jnp.zeros((panels, 3 * RANK), F32)
    minus = -area[:, :RANK]
    scaled_ref[...] = jnp.concatenate(
        [gap, minus * spread, gap, minus * upper_left], axis=1
    ).astype(BF16)
    sources = count_ref.shape[1]
    slots = target_ref.shape[1]
    counts = jnp.broadcast_to(count_ref[...].astype(F32), (16, sources)).astype(BF16)
    source = lax.broadcasted_iota(I32, (sources, slots), 0)
    column = lax.broadcasted_iota(I32, (sources, slots), 1) // SLOT_ROWS
    start = mm(counts, jnp.where(source < column, 1.0, 0.0).astype(BF16))[0:1]
    mine = mm(counts, jnp.where(source == column, 1.0, 0.0).astype(BF16))[0:1]
    slot = lax.broadcasted_iota(I32, (1, slots), 1) % SLOT_ROWS - 4 * place_ref[3]
    slot = slot.astype(F32)
    target_ref[...] = jnp.where((slot >= 0.0) & (slot < mine), start + slot, -1.0)


def prepare(place, rank, count, diag, lower, right, upper, back, area):
    panels, slots = diag.shape[0], count.shape[1] * SLOT_ROWS
    return pl.pallas_call(
        prepare_kernel,
        in_specs=[SMEM, SMEM] + [VMEM] * 7,
        out_specs=[VMEM] * 5,
        out_shape=[
            jax.ShapeDtypeStruct((panels, 4 * RANK), BF16),
            jax.ShapeDtypeStruct((2 * RANK, 4 * RANK), BF16),
            jax.ShapeDtypeStruct((1, slots), F32),
            jax.ShapeDtypeStruct((panels, 8 * RANK), BF16),
            jax.ShapeDtypeStruct((panels, 4 * RANK), F32),
        ],
        compiler_params=PARAMS,
        cost_estimate=pl.CostEstimate(
            flops=4 << 30, bytes_accessed=8 << 20, transcendentals=0
        ),
    )(place, rank, count, diag, lower, right, upper, back, area)


def select_kernel(arrived_ref, target_ref, normal_ref, turned_ref):
    panels, width = normal_ref.shape
    target = target_ref[...]
    sources = target.shape[1] // SLOT_ROWS
    step = 256
    parts = []
    for begin in range(0, panels, step):
        least = max(0, (begin - CAP + 1) // CAP)
        most = min(sources, (begin + step - 1 + CAP * sources - panels) // CAP + 1)
        first = least * SLOT_ROWS // 128 * 128
        last = -(-most * SLOT_ROWS // 128) * 128
        panel = (lax.broadcasted_iota(I32, (step, last - first), 0) + begin).astype(F32)
        pick = jnp.where(panel == target[:, first:last], 1.0, 0.0).astype(BF16)
        parts.append(mm(pick, arrived_ref[first:last, :]).astype(BF16))
    normal = jnp.concatenate(parts, axis=0)
    normal_ref[...] = normal
    row = lax.broadcasted_iota(I32, (width, width), 0)
    mode = (row % 16) // 2 * 16 + row // 16 * 2 + row % 2
    order = jnp.where(lax.broadcasted_iota(I32, (width, width), 1) == mode, 1.0, 0.0)
    turned_ref[...] = mm_t(order.astype(BF16), normal).astype(BF16)


def select(arrived, target, panels):
    width = arrived.shape[1]
    return pl.pallas_call(
        select_kernel,
        in_specs=[VMEM] * 2,
        out_specs=[VMEM] * 2,
        out_shape=[
            jax.ShapeDtypeStruct((panels, width), BF16),
            jax.ShapeDtypeStruct((width, panels), BF16),
        ],
        compiler_params=PARAMS,
        cost_estimate=pl.CostEstimate(
            flops=1 << 29, bytes_accessed=2 << 20, transcendentals=0
        ),
    )(arrived, target)


def solve_kernel(normal_ref, diag_ref, right_ref, back_ref, solved_ref, seen_ref):
    solved = mm(diag_ref[...], normal_ref[...])
    solved_ref[...] = solved
    high, low = halves(solved)
    width = solved.shape[1]
    both = jnp.concatenate([right_ref[...], back_ref[...]], axis=0)
    seen = mm(both, jnp.concatenate([high, low], axis=1))
    seen_ref[...] = (seen[:, :width] + seen[:, width:]).astype(BF16)


def solve(normal, diag, right, back):
    panels, width = normal.shape
    return pl.pallas_call(
        solve_kernel,
        in_specs=[VMEM] * 4,
        out_specs=[VMEM] * 2,
        out_shape=[
            jax.ShapeDtypeStruct((panels, width), F32),
            jax.ShapeDtypeStruct((2 * RANK, width), BF16),
        ],
        compiler_params=PARAMS,
        cost_estimate=pl.CostEstimate(
            flops=1 << 29, bytes_accessed=4 << 20, transcendentals=0
        ),
    )(normal, diag, right, back)


def local_kernel(
    place_ref, solved_ref, scaled_ref, area_ref, turned_ref, other_ref, seen_ref, mats_ref,
    send_ref,
):
    width = solved_ref.shape[1]
    peers = send_ref.shape[0]
    part = width // peers
    weighted = (area_ref[...] * solved_ref[...]).astype(BF16)
    factor = jnp.concatenate([weighted, scaled_ref[...]], axis=1)
    own = mm(turned_ref[...], factor)
    other = mm(other_ref[...], factor)
    even = place_ref[2] == 0
    send_ref[:, 0 : 2 * RANK, :] = jnp.broadcast_to(
        seen_ref[...][None], (peers, 2 * RANK, width)
    )
    mats = mats_ref[...].astype(F32)
    for side in range(2):
        rows = jnp.where(even, other, own) if side else jnp.where(even, own, other)
        begin = 4 * RANK + side * part
        fixed = rows[:, :width].astype(BF16)
        send_ref[:, begin : begin + part, :] = fixed.reshape(peers, part, width)
        for which in range(2):
            begin = which * RANK + side * part
            block = rows[:, (1 + which) * width : (2 + which) * width].reshape(peers, part, width)
            block = (block + mats[begin : begin + part][None]).astype(BF16)
            send_ref[:, 2 * RANK + begin : 2 * RANK + begin + part, :] = block


def local(place, solved, scaled, area, turned, other, seen, mats, peers):
    width = solved.shape[1]
    return pl.pallas_call(
        local_kernel,
        in_specs=[SMEM] + [VMEM] * 7,
        out_specs=VMEM,
        out_shape=jax.ShapeDtypeStruct((peers, 5 * RANK, width), BF16),
        compiler_params=PARAMS,
        cost_estimate=pl.CostEstimate(
            flops=1 << 28, bytes_accessed=2 << 20, transcendentals=0
        ),
    )(place, solved, scaled, area, turned, other, seen, mats)


def element(ref, position):
    high = ref[position, 2 * RANK : 3 * RANK, :]
    low = ref[position, 3 * RANK : 4 * RANK, :]

    def wide(which):
        lanes = slice(which * RANK, (which + 1) * RANK)
        return jnp.concatenate([high[:, lanes], low[:, lanes], high[:, lanes]], axis=1)

    vectors = ref[position, 0 : 2 * RANK, :].astype(F32)
    back = high[:, RANK : 2 * RANK].astype(F32) + low[:, RANK : 2 * RANK].astype(F32)
    return vectors[:RANK], vectors[RANK:], [wide(0), wide(2)], back


def gain_step(total, mask, middle):
    factor = total[:, TURN : TURN + RANK]
    if mask is not None:
        factor = factor * mask
    high, low = halves(factor)
    middle_high, middle_low = halves(middle)
    rows = factor.shape[0]
    first = mm(jnp.concatenate([high, low], axis=0), middle_high)
    return total + (first[:rows] + first[rows:] + mm(high, middle_low))


def unit(offset):
    row = lax.broadcasted_iota(I32, (RANK, WIDE), 0)
    lane = lax.broadcasted_iota(I32, (RANK, WIDE), 1)
    return jnp.where(lane == row + offset, 1.0, 0.0).astype(F32)


def advance(forward, total, parts, mask):
    shift, gain, ahead, back, by_s, by_t, fixed = parts
    width = fixed.shape[1]
    pad = jnp.zeros((RANK, WIDE - width), F32)
    gap, tail = jnp.zeros((RANK, width), F32), jnp.zeros((RANK, WIDE - width - RANK), F32)
    moved = mm(jnp.concatenate(ahead + [by_s], axis=0), tall(forward))
    later = forward + moved[:RANK] + jnp.concatenate([shift, pad], axis=1)
    middle = (
        jnp.concatenate([gain, pad], axis=1)
        + jnp.concatenate([gap, back, tail], axis=1)
        - moved[RANK : 2 * RANK]
    )
    mass = moved[2 * RANK :] + jnp.concatenate([fixed, by_t, tail[: fixed.shape[0]]], axis=1)
    none = jnp.zeros((2 * RANK, WIDE), F32)
    total = gain_step(total, mask, middle) + jnp.concatenate([none, mass], axis=0)
    return later, total


def own_mask(rows, keep):
    row = lax.broadcasted_iota(I32, (rows, RANK), 0)
    return jnp.where((row >= RANK) & (row < 2 * RANK) & jnp.logical_not(keep), 0.0, 1.0)


def start_total(rows):
    head = [unit(TURN), unit(TURN)]
    return jnp.concatenate(head + [jnp.zeros((rows, WIDE), F32)], axis=0)


def inner_kernel(place_ref, got_ref, own_ref, send_ref):
    width = got_ref.shape[2]
    mine = place_ref[0]
    in_t, in_s = TURN, TURN + RANK
    forward, total = unit(in_s), start_total(RANK)
    own_s = jnp.zeros_like(forward)
    blank = jnp.zeros((RANK, RANK), BF16)
    for position in range(got_ref.shape[0]):
        by_s = got_ref[position, 2 * RANK : 3 * RANK, 3 * RANK : 4 * RANK]
        by_t = got_ref[position, 3 * RANK : 4 * RANK, 3 * RANK : 4 * RANK].astype(F32)
        fixed = got_ref[position, 4 * RANK : 5 * RANK, :].astype(F32)
        by_s = jnp.concatenate([by_s, blank, by_s], axis=1)
        own_s = jnp.where(mine == position, forward, own_s)
        forward, total = advance(
            forward, total, element(got_ref, position) + (by_s, by_t, fixed),
            own_mask(3 * RANK, position > mine),
        )
    own_ref[...] = jnp.concatenate([own_s, total[RANK : 2 * RANK]], axis=0)
    eye = unit(0)[:, :RANK]
    mats = jnp.concatenate(
        [
            forward[:, in_s : in_s + RANK] - eye,
            total[:RANK, in_t : in_t + RANK] - eye,
            -total[:RANK, in_s : in_s + RANK],
            jnp.zeros((RANK, RANK), F32),
        ],
        axis=1,
    )
    high, low = halves(mats)
    message = jnp.concatenate(
        [forward[:, :width].astype(BF16), total[:RANK, :width].astype(BF16), high, low], axis=0
    )
    peers = send_ref.shape[0]
    send_ref[:, 0 : 4 * RANK, :] = jnp.broadcast_to(message[None], (peers, 4 * RANK, width))
    mass = total[2 * RANK :]
    fixed_high, fixed_low = halves(mass[:, :width])
    by_s_high, by_s_low = halves(mass[:, in_s : in_s + RANK])
    by_t_high, by_t_low = halves(mass[:, in_t : in_t + RANK])
    maps = jnp.concatenate([by_s_high, by_s_low, by_t_high, by_t_low], axis=1)
    sources = jnp.concatenate([fixed_high, fixed_low, maps, jnp.zeros_like(maps)], axis=0)
    row = lax.broadcasted_iota(I32, (peers * 16, 4 * RANK), 0)
    column = lax.broadcasted_iota(I32, (peers * 16, 4 * RANK), 1)
    slot = row % 16
    block = jnp.where(slot < 4, slot // 2, jnp.where((slot == 8) | (slot == 9), 2, 3))
    pick = jnp.where(column == block * RANK + row // 16 * 2 + slot % 2, 1.0, 0.0).astype(BF16)
    send_ref[:, 4 * RANK :, :] = mm(pick, sources).astype(BF16).reshape(peers, 16, width)


def inner(place, got, peers):
    return pl.pallas_call(
        inner_kernel,
        in_specs=[SMEM, VMEM],
        out_specs=[VMEM] * 2,
        out_shape=[
            jax.ShapeDtypeStruct((2 * RANK, WIDE), F32),
            jax.ShapeDtypeStruct((peers, 4 * RANK + 16, got.shape[2]), BF16),
        ],
        compiler_params=PARAMS,
    )(place, got)


def outer_kernel(
    place_ref, got_ref, own_ref, solved_ref, stack_ref, potential_ref, mass_ref,
):
    width = got_ref.shape[2]
    groups = GROUPS
    members = got_ref.shape[0] // groups
    my_group, my_member = place_ref[1] // members, place_ref[1] % members
    in_t, in_s = TURN, TURN + RANK
    forwards = [unit(in_s)] * groups
    totals = [start_total(16)] * groups
    own_s = jnp.zeros((RANK, WIDE), F32)
    zero8 = jnp.zeros((8, 4 * RANK), F32)
    for member in range(members):
        mask = own_mask(2 * RANK + 16, member > my_member)
        for group in range(groups):
            position = group * members + member
            fixed = got_ref[position, 4 * RANK :, :].astype(F32)
            maps = jnp.concatenate([fixed[8:16], zero8], axis=0)
            by_s = maps[:, :RANK].astype(BF16)
            by_s = jnp.concatenate(
                [by_s, maps[:, RANK : 2 * RANK].astype(BF16), by_s], axis=1
            )
            by_t = maps[:, 2 * RANK : 3 * RANK] + maps[:, 3 * RANK :]
            here = (my_group == group) & (my_member == member)
            own_s = jnp.where(here, forwards[group], own_s)
            forwards[group], totals[group] = advance(
                forwards[group], totals[group],
                element(got_ref, position) + (by_s, by_t, fixed), mask,
            )
    own_t = jnp.zeros((RANK, WIDE), F32)
    for group in range(groups):
        own_t = jnp.where(my_group == group, totals[group][RANK : 2 * RANK], own_t)
    own = own_ref[...]
    map_high, map_low = halves(own[:, width : width + 2 * RANK])
    maps = jnp.concatenate([map_high, map_low, map_high], axis=1)
    lanes = lax.broadcasted_iota(I32, own.shape, 1)
    own = jnp.where(lanes < width, own, 0.0) + mm(
        maps, tall(jnp.concatenate([own_t, own_s], axis=0))
    )
    eye = unit(0)[:, :RANK]
    forward = jnp.zeros((RANK, width), F32)
    enter_s = forward
    total = jnp.concatenate([unit(TURN), jnp.zeros((16, WIDE), F32)], axis=0)
    none, rest = jnp.zeros((RANK, WIDE), F32), jnp.zeros((RANK, WIDE - width - RANK), F32)
    row = lax.broadcasted_iota(I32, (RANK + 16, RANK), 0)
    for group in range(groups):
        step, whole = forwards[group], totals[group]
        mass = whole[2 * RANK :]
        ahead = jnp.concatenate(
            [
                step[:, in_s : in_s + RANK] - eye,
                whole[:RANK, in_s : in_s + RANK],
                mass[:, in_s : in_s + RANK],
            ],
            axis=0,
        )
        high, low = halves(ahead)
        enter_s = jnp.where(my_group == group, forward, enter_s)
        moved = mm(jnp.concatenate([high, low, high], axis=1), tall(forward))
        forward = forward + moved[:RANK] + step[:, :width]
        middle = jnp.concatenate(
            [
                whole[:RANK, :width] + moved[RANK : 2 * RANK],
                whole[:RANK, in_t : in_t + RANK] - eye,
                rest,
            ],
            axis=1,
        )
        mask = jnp.where((row < RANK) & (group <= my_group), 0.0, 1.0)
        mass = jnp.concatenate(
            [mass[:, :width] + moved[2 * RANK :], mass[:, in_t : in_t + RANK], rest[:16]], axis=1
        )
        total = gain_step(total, mask, middle) + jnp.concatenate([none, mass], axis=0)
    enter_t = total[:RANK, :width]
    mass = total[RANK:, :width]
    mass_ref[...] = mass[0:2] + mass[2:4]
    map_high, map_low = halves(own[:, width : width + 2 * RANK])
    maps = jnp.concatenate([map_high, map_low, map_high], axis=1)
    state = own[:, :width] + mm(maps, tall(jnp.concatenate([enter_t, enter_s], axis=0)))
    high, low = halves(state)
    blank = jnp.zeros((RANK, width), BF16)
    left = jnp.concatenate([high, high[:RANK], blank], axis=0)
    right = jnp.concatenate([low, blank, blank], axis=0)
    fixed = mm(stack_ref[...], jnp.concatenate([left, right], axis=1))
    potential = solved_ref[...] - (fixed[:, :width] + fixed[:, width:])
    potential_ref[...] = potential.astype(BF16)


def outer(place, got, own, solved, stack):
    panels, width = solved.shape
    return pl.pallas_call(
        outer_kernel,
        in_specs=[SMEM] + [VMEM] * 4,
        out_specs=[VMEM] * 2,
        out_shape=[
            jax.ShapeDtypeStruct((panels, width), BF16),
            jax.ShapeDtypeStruct((2, width), F32),
        ],
        compiler_params=PARAMS,
    )(place, got, own, solved, stack)


def body(
    node_modes, node_index, interp, normals, counts, inverse_diag,
    lower_left, lower_right, upper_left, upper_right, ranks, areas,
):
    devices, width = lax.axis_size(AXES), node_modes.shape[2]
    inner_size, outer_size = lax.axis_size("z"), lax.axis_size(("y", "x"))
    depth, group = lax.axis_index("z"), lax.axis_index(("y", "x"))
    place = jnp.stack([depth, group, lax.axis_index("side"), depth % 2]).astype(I32)
    outgoing = interpolate(node_modes, node_index, interp, normals)
    arrived = lax.all_to_all(
        outgoing.reshape(devices, SLOT_ROWS, width), AXES, split_axis=0, concat_axis=0, tiled=True
    ).reshape(devices * SLOT_ROWS, width)
    right, back = lower_right.T, upper_right.T
    stack, mats, target, scaled, area = prepare(
        place, ranks, counts.reshape(1, devices), inverse_diag, lower_left.T, right,
        upper_left.T, back, areas.reshape(1, -1),
    )
    normal, turned = select(arrived, target, inverse_diag.shape[0])
    other = lax.ppermute(turned, "side", [(0, 1), (1, 0)])
    solved, seen = solve(normal, inverse_diag, right, back)
    send = local(place, solved, scaled, area, turned, other, seen, mats, inner_size)
    got = lax.all_to_all(send, "z", split_axis=0, concat_axis=0, tiled=True)
    own, send = inner(place, got, outer_size)
    got = lax.all_to_all(send, ("y", "x"), split_axis=0, concat_axis=0, tiled=True)
    return outer(place, got, own, solved, stack)


def solution(mesh):
    grid = jax.sharding.Mesh(mesh.devices.reshape(2, 4, 4, 8), ("side",) + AXES)
    in_specs = (
        P(None, AXES, "side"),
        P(None, AXES),
        P(None, AXES),
        P(None, AXES),
        P(None, AXES),
        P(AXES, None),
        P(AXES, None),
        P(AXES, None),
        P(AXES, None),
        P(AXES, None),
        P(AXES),
        P(AXES),
    )
    out_specs = (P(AXES, "side"), P(AXES, "side"))
    return jax.shard_map(body, mesh=grid, in_specs=in_specs, out_specs=out_specs, check_vma=False)
```

```python
import functools
import jax
import jax.numpy as jnp
from jax import lax
from jax.experimental import pallas as pl
from jax.experimental.pallas import tpu as pltpu
from jax.sharding import PartitionSpec as P

F32, BF16, I32 = jnp.float32, jnp.bfloat16, jnp.int32
AXES = ("y", "x", "z")
RANK, CAP, SLOT_ROWS, WIDE = 32, 12, 16, 256
PARAMS = pltpu.CompilerParams(vmem_limit_bytes=28 * 1024 * 1024)
WHOLE = pltpu.CompilerParams(vmem_limit_bytes=62 * 1024 * 1024)
VMEM = pl.BlockSpec(memory_space=pltpu.VMEM)
SMEM = pl.BlockSpec(memory_space=pltpu.SMEM)
HBM = pl.BlockSpec(memory_space=pltpu.HBM)
STEPS, TURN, GROUPS = 4, 128, 4
TILE, LANES, ROWS = 32, 256, 192


def mm(a, b):
    return lax.dot_general(a, b, (((1,), (0,)), ((), ())), preferred_element_type=F32)


def mm_t(a, b):
    return lax.dot_general(a, b, (((1,), (1,)), ((), ())), preferred_element_type=F32)


def halves(value):
    high = value.astype(BF16)
    return high, (value - high.astype(F32)).astype(BF16)


def tall(value):
    high, low = halves(value)
    return jnp.concatenate([high, high, low], axis=0)


def interp_kernel(
    modes_hbm, index_hbm, interp_hbm, normals_hbm, out_hbm,
    modes_ref, index_ref, interp_ref, normals_ref, high_ref, low_ref, out_ref, sems, out_sems,
):
    pairs = [
        (index_hbm, index_ref), (interp_hbm, interp_ref), (normals_hbm, normals_ref),
        (modes_hbm, modes_ref),
    ]
    copies = [
        pltpu.make_async_copy(source, target, sems.at[number])
        for number, (source, target) in enumerate(pairs)
    ]
    for copy in copies:
        copy.start()
    for copy in copies[:3]:
        copy.wait()
    slots, nodes = index_ref.shape[1], modes_ref.shape[1]
    width = modes_ref.shape[2]
    chunk = slots // STEPS
    node = lax.broadcasted_iota(I32, (TILE, nodes), 1).astype(F32)
    leaving = []
    for step in range(STEPS):
        lanes = slice(step * chunk, (step + 1) * chunk)
        rows = jnp.concatenate(
            [
                index_ref[:, lanes].astype(F32),
                interp_ref[:, lanes],
                normals_ref[:, lanes],
                jnp.zeros((5, chunk), F32),
            ],
            axis=0,
        )
        columns = rows.T
        if step == 0:
            copies[3].wait()
        for begin in range(0, chunk, TILE):
            part = columns[begin : begin + TILE]
            for lane in range(0, nodes, LANES):
                mix = jnp.zeros((TILE, LANES), F32)
                for corner in range(4):
                    here = part[:, corner : corner + 1] == node[:, lane : lane + LANES]
                    mix = mix + jnp.where(here, part[:, 4 + corner : 5 + corner], 0.0)
                high, low = halves(mix)
                high_ref[step % 2, begin : begin + TILE, lane : lane + LANES] = high
                low_ref[step % 2, begin : begin + TILE, lane : lane + LANES] = low
        table = jnp.concatenate([modes_ref[0], modes_ref[1], modes_ref[2]], axis=1)
        for begin in range(0, chunk, ROWS):
            picked = mm(high_ref[step % 2, begin : begin + ROWS], table) + mm(
                low_ref[step % 2, begin : begin + ROWS], table
            )
            velocity = jnp.zeros((ROWS, width), F32)
            for axis_id in range(3):
                part = picked[:, axis_id * width : (axis_id + 1) * width]
                normal = columns[begin : begin + ROWS, 8 + axis_id : 9 + axis_id]
                velocity = velocity + normal * part
            blocks = velocity.reshape(ROWS // 24, 24, width)
            where = slice((step * chunk + begin) // 24, (step * chunk + begin + ROWS) // 24)
            out_ref[where, 0:16, :] = blocks[:, 0:16, :].astype(BF16)
            out_ref[where, 16:32, :] = blocks[:, 8:24, :].astype(BF16)
        where = pl.ds(step * chunk // 24, chunk // 24)
        leaving.append(
            pltpu.make_async_copy(out_ref.at[where], out_hbm.at[where], out_sems.at[step])
        )
        leaving[-1].start()
    for copy in leaving:
        copy.wait()


def interpolate(node_modes, node_index, interp, normals):
    slots, width = node_index.shape[1], node_modes.shape[2]
    return pl.pallas_call(
        interp_kernel,
        in_specs=[HBM] * 4,
        out_specs=HBM,
        out_shape=jax.ShapeDtypeStruct((slots // 24, 32, width), BF16),
        scratch_shapes=[
            pltpu.VMEM(node_modes.shape, BF16),
            pltpu.VMEM(node_index.shape, I32),
            pltpu.VMEM(interp.shape, F32),
            pltpu.VMEM(normals.shape, F32),
            pltpu.VMEM((2, slots // STEPS, node_modes.shape[1]), BF16),
            pltpu.VMEM((2, slots // STEPS, node_modes.shape[1]), BF16),
            pltpu.VMEM((slots // 24, 32, width), BF16),
            pltpu.SemaphoreType.DMA((4,)),
            pltpu.SemaphoreType.DMA((STEPS,)),
        ],
        compiler_params=WHOLE,
        cost_estimate=pl.CostEstimate(
            flops=2 * slots * 1024 * 384, bytes_accessed=1 << 20, transcendentals=0
        ),
    )(node_modes, node_index, interp, normals)


def prepare_kernel(
    place_ref, rank_ref, count_ref, diag_ref, lower_ref, right_ref, upper_ref, back_ref, area_ref,
    stack_ref, mats_ref, target_ref, scaled_ref, area_out_ref,
):
    panels = diag_ref.shape[0]
    keep = lax.broadcasted_iota(I32, (RANK, panels), 0) < rank_ref[0]
    zero = jnp.zeros((RANK, panels), BF16)
    lower = jnp.where(keep, lower_ref[...], zero)
    upper = jnp.where(keep, upper_ref[...], zero)
    spread = mm_t(diag_ref[...], lower)
    high, low = halves(spread)
    both = jnp.concatenate([right_ref[...], back_ref[...]], axis=0)
    seen = mm(both, jnp.concatenate([high, low], axis=1))
    seen = seen[:, :RANK] + seen[:, RANK:]
    back = mm_t(back_ref[...], upper)
    blank = jnp.zeros((RANK, RANK), F32)
    mats = jnp.concatenate([-seen[:RANK], -back, seen[RANK:], blank], axis=1)
    mats_high, mats_low = halves(mats)
    mats_ref[...] = jnp.concatenate([mats_high, mats_low], axis=0)
    upper_left = upper.astype(F32).T
    stack_ref[...] = jnp.concatenate(
        [high, upper_left.astype(BF16), low, jnp.zeros((panels, RANK), BF16)], axis=1
    )
    area = jnp.broadcast_to(jnp.broadcast_to(area_ref[...], (8, panels)).T[:, 0:1], (panels, 128))
    area_out_ref[...] = area
    gap = jnp.zeros((panels, 3 * RANK), F32)
    minus = -area[:, :RANK]
    scaled_ref[...] = jnp.concatenate(
        [gap, minus * spread, gap, minus * upper_left], axis=1
    ).astype(BF16)
    sources = count_ref.shape[1]
    slots = target_ref.shape[1]
    counts = jnp.broadcast_to(count_ref[...].astype(F32), (16, sources)).astype(BF16)
    source = lax.broadcasted_iota(I32, (sources, slots), 0)
    column = lax.broadcasted_iota(I32, (sources, slots), 1) // SLOT_ROWS
    start = mm(counts, jnp.where(source < column, 1.0, 0.0).astype(BF16))[0:1]
    mine = mm(counts, jnp.where(source == column, 1.0, 0.0).astype(BF16))[0:1]
    slot = lax.broadcasted_iota(I32, (1, slots), 1) % SLOT_ROWS - 4 * place_ref[3]
    slot = slot.astype(F32)
    target_ref[...] = jnp.where((slot >= 0.0) & (slot < mine), start + slot, -1.0)


def prepare(place, rank, count, diag, lower, right, upper, back, area):
    panels, slots = diag.shape[0], count.shape[1] * SLOT_ROWS
    return pl.pallas_call(
        prepare_kernel,
        in_specs=[SMEM, SMEM] + [VMEM] * 7,
        out_specs=[VMEM] * 5,
        out_shape=[
            jax.ShapeDtypeStruct((panels, 4 * RANK), BF16),
            jax.ShapeDtypeStruct((2 * RANK, 4 * RANK), BF16),
            jax.ShapeDtypeStruct((1, slots), F32),
            jax.ShapeDtypeStruct((panels, 8 * RANK), BF16),
            jax.ShapeDtypeStruct((panels, 4 * RANK), F32),
        ],
        compiler_params=PARAMS,
        cost_estimate=pl.CostEstimate(
            flops=4 << 30, bytes_accessed=8 << 20, transcendentals=0
        ),
    )(place, rank, count, diag, lower, right, upper, back, area)


def select_kernel(arrived_ref, target_ref, normal_ref, turned_ref):
    panels, width = normal_ref.shape
    target = target_ref[...]
    sources = target.shape[1] // SLOT_ROWS
    step = 256
    parts = []
    for begin in range(0, panels, step):
        least = max(0, (begin - CAP + 1) // CAP)
        most = min(sources, (begin + step - 1 + CAP * sources - panels) // CAP + 1)
        first = least * SLOT_ROWS // 128 * 128
        last = -(-most * SLOT_ROWS // 128) * 128
        panel = (lax.broadcasted_iota(I32, (step, last - first), 0) + begin).astype(F32)
        pick = jnp.where(panel == target[:, first:last], 1.0, 0.0).astype(BF16)
        parts.append(mm(pick, arrived_ref[first:last, :]).astype(BF16))
    normal = jnp.concatenate(parts, axis=0)
    normal_ref[...] = normal
    row = lax.broadcasted_iota(I32, (width, width), 0)
    mode = (row % 16) // 2 * 16 + row // 16 * 2 + row % 2
    order = jnp.where(lax.broadcasted_iota(I32, (width, width), 1) == mode, 1.0, 0.0)
    turned_ref[...] = mm_t(order.astype(BF16), normal).astype(BF16)


def select(arrived, target, panels):
    width = arrived.shape[1]
    return pl.pallas_call(
        select_kernel,
        in_specs=[VMEM] * 2,
        out_specs=[VMEM] * 2,
        out_shape=[
            jax.ShapeDtypeStruct((panels, width), BF16),
            jax.ShapeDtypeStruct((width, panels), BF16),
        ],
        compiler_params=PARAMS,
        cost_estimate=pl.CostEstimate(
            flops=1 << 29, bytes_accessed=2 << 20, transcendentals=0
        ),
    )(arrived, target)


def solve_kernel(normal_ref, diag_ref, right_ref, back_ref, solved_ref, seen_ref):
    solved = mm(diag_ref[...], normal_ref[...])
    solved_ref[...] = solved
    high, low = halves(solved)
    width = solved.shape[1]
    both = jnp.concatenate([right_ref[...], back_ref[...]], axis=0)
    seen = mm(both, jnp.concatenate([high, low], axis=1))
    seen_ref[...] = (seen[:, :width] + seen[:, width:]).astype(BF16)


def solve(normal, diag, right, back):
    panels, width = normal.shape
    return pl.pallas_call(
        solve_kernel,
        in_specs=[VMEM] * 4,
        out_specs=[VMEM] * 2,
        out_shape=[
            jax.ShapeDtypeStruct((panels, width), F32),
            jax.ShapeDtypeStruct((2 * RANK, width), BF16),
        ],
        compiler_params=PARAMS,
        cost_estimate=pl.CostEstimate(
            flops=1 << 29, bytes_accessed=4 << 20, transcendentals=0
        ),
    )(normal, diag, right, back)


def local_kernel(
    place_ref, solved_ref, scaled_ref, area_ref, turned_ref, other_ref, seen_ref, mats_ref,
    send_ref,
):
    width = solved_ref.shape[1]
    peers = send_ref.shape[0]
    part = width // peers
    weighted = (area_ref[...] * solved_ref[...]).astype(BF16)
    factor = jnp.concatenate([weighted, scaled_ref[...]], axis=1)
    own = mm(turned_ref[...], factor)
    other = mm(other_ref[...], factor)
    even = place_ref[2] == 0
    send_ref[:, 0 : 2 * RANK, :] = jnp.broadcast_to(
        seen_ref[...][None], (peers, 2 * RANK, width)
    )
    mats = mats_ref[...].astype(F32)
    for side in range(2):
        rows = jnp.where(even, other, own) if side else jnp.where(even, own, other)
        begin = 4 * RANK + side * part
        fixed = rows[:, :width].astype(BF16)
        send_ref[:, begin : begin + part, :] = fixed.reshape(peers, part, width)
        for which in range(2):
            begin = which * RANK + side * part
            block = rows[:, (1 + which) * width : (2 + which) * width].reshape(peers, part, width)
            block = (block + mats[begin : begin + part][None]).astype(BF16)
            send_ref[:, 2 * RANK + begin : 2 * RANK + begin + part, :] = block


def local(place, solved, scaled, area, turned, other, seen, mats, peers):
    width = solved.shape[1]
    return pl.pallas_call(
        local_kernel,
        in_specs=[SMEM] + [VMEM] * 7,
        out_specs=VMEM,
        out_shape=jax.ShapeDtypeStruct((peers, 5 * RANK, width), BF16),
        compiler_params=PARAMS,
        cost_estimate=pl.CostEstimate(
            flops=1 << 28, bytes_accessed=2 << 20, transcendentals=0
        ),
    )(place, solved, scaled, area, turned, other, seen, mats)


def element(ref, position):
    high = ref[position, 2 * RANK : 3 * RANK, :]
    low = ref[position, 3 * RANK : 4 * RANK, :]

    def wide(which):
        lanes = slice(which * RANK, (which + 1) * RANK)
        return jnp.concatenate([high[:, lanes], low[:, lanes], high[:, lanes]], axis=1)

    vectors = ref[position, 0 : 2 * RANK, :].astype(F32)
    back = high[:, RANK : 2 * RANK].astype(F32) + low[:, RANK : 2 * RANK].astype(F32)
    return vectors[:RANK], vectors[RANK:], [wide(0), wide(2)], back


def gain_step(total, mask, middle):
    factor = total[:, TURN : TURN + RANK]
    if mask is not None:
        factor = factor * mask
    high, low = halves(factor)
    return total + mm(jnp.concatenate([high, low, high], axis=1), tall(middle))


def unit(offset):
    row = lax.broadcasted_iota(I32, (RANK, WIDE), 0)
    lane = lax.broadcasted_iota(I32, (RANK, WIDE), 1)
    return jnp.where(lane == row + offset, 1.0, 0.0).astype(F32)


def advance(forward, total, parts, mask):
    shift, gain, ahead, back, by_s, by_t, fixed = parts
    width = fixed.shape[1]
    pad = jnp.zeros((RANK, WIDE - width), F32)
    gap, tail = jnp.zeros((RANK, width), F32), jnp.zeros((RANK, WIDE - width - RANK), F32)
    moved = mm(jnp.concatenate(ahead + [by_s], axis=0), tall(forward))
    later = forward + moved[:RANK] + jnp.concatenate([shift, pad], axis=1)
    middle = (
        jnp.concatenate([gain, pad], axis=1)
        + jnp.concatenate([gap, back, tail], axis=1)
        - moved[RANK : 2 * RANK]
    )
    mass = moved[2 * RANK :] + jnp.concatenate([fixed, by_t, tail[: fixed.shape[0]]], axis=1)
    none = jnp.zeros((2 * RANK, WIDE), F32)
    total = gain_step(total, mask, middle) + jnp.concatenate([none, mass], axis=0)
    return later, total


def own_mask(rows, keep):
    row = lax.broadcasted_iota(I32, (rows, RANK), 0)
    return jnp.where((row >= RANK) & (row < 2 * RANK) & jnp.logical_not(keep), 0.0, 1.0)


def start_total(rows):
    head = [unit(TURN), unit(TURN)]
    return jnp.concatenate(head + [jnp.zeros((rows, WIDE), F32)], axis=0)


def inner_kernel(place_ref, got_ref, own_ref, send_ref):
    width = got_ref.shape[2]
    mine = place_ref[0]
    in_t, in_s = TURN, TURN + RANK
    forward, total = unit(in_s), start_total(RANK)
    own_s = jnp.zeros_like(forward)
    blank = jnp.zeros((RANK, RANK), BF16)
    for position in range(got_ref.shape[0]):
        by_s = got_ref[position, 2 * RANK : 3 * RANK, 3 * RANK : 4 * RANK]
        by_t = got_ref[position, 3 * RANK : 4 * RANK, 3 * RANK : 4 * RANK].astype(F32)
        fixed = got_ref[position, 4 * RANK : 5 * RANK, :].astype(F32)
        by_s = jnp.concatenate([by_s, blank, by_s], axis=1)
        own_s = jnp.where(mine == position, forward, own_s)
        forward, total = advance(
            forward, total, element(got_ref, position) + (by_s, by_t, fixed),
            own_mask(3 * RANK, position > mine),
        )
    own_ref[...] = jnp.concatenate([own_s, total[RANK : 2 * RANK]], axis=0)
    eye = unit(0)[:, :RANK]
    mats = jnp.concatenate(
        [
            forward[:, in_s : in_s + RANK] - eye,
            total[:RANK, in_t : in_t + RANK] - eye,
            -total[:RANK, in_s : in_s + RANK],
            jnp.zeros((RANK, RANK), F32),
        ],
        axis=1,
    )
    high, low = halves(mats)
    message = jnp.concatenate(
        [forward[:, :width].astype(BF16), total[:RANK, :width].astype(BF16), high, low], axis=0
    )
    peers = send_ref.shape[0]
    send_ref[:, 0 : 4 * RANK, :] = jnp.broadcast_to(message[None], (peers, 4 * RANK, width))
    mass = total[2 * RANK :]
    fixed_high, fixed_low = halves(mass[:, :width])
    by_s_high, by_s_low = halves(mass[:, in_s : in_s + RANK])
    by_t_high, by_t_low = halves(mass[:, in_t : in_t + RANK])
    maps = jnp.concatenate([by_s_high, by_s_low, by_t_high, by_t_low], axis=1)
    sources = jnp.concatenate([fixed_high, fixed_low, maps, jnp.zeros_like(maps)], axis=0)
    row = lax.broadcasted_iota(I32, (peers * 16, 4 * RANK), 0)
    column = lax.broadcasted_iota(I32, (peers * 16, 4 * RANK), 1)
    slot = row % 16
    block = jnp.where(slot < 4, slot // 2, jnp.where((slot == 8) | (slot == 9), 2, 3))
    pick = jnp.where(column == block * RANK + row // 16 * 2 + slot % 2, 1.0, 0.0).astype(BF16)
    send_ref[:, 4 * RANK :, :] = mm(pick, sources).astype(BF16).reshape(peers, 16, width)


def inner(place, got, peers):
    return pl.pallas_call(
        inner_kernel,
        in_specs=[SMEM, VMEM],
        out_specs=[VMEM] * 2,
        out_shape=[
            jax.ShapeDtypeStruct((2 * RANK, WIDE), F32),
            jax.ShapeDtypeStruct((peers, 4 * RANK + 16, got.shape[2]), BF16),
        ],
        compiler_params=PARAMS,
    )(place, got)


def outer_kernel(
    place_ref, got_ref, own_ref, solved_ref, stack_ref, potential_ref, mass_ref,
):
    width = got_ref.shape[2]
    groups = GROUPS
    members = got_ref.shape[0] // groups
    my_group, my_member = place_ref[1] // members, place_ref[1] % members
    in_t, in_s = TURN, TURN + RANK
    forwards = [unit(in_s)] * groups
    totals = [start_total(16)] * groups
    own_s = jnp.zeros((RANK, WIDE), F32)
    zero8 = jnp.zeros((8, 4 * RANK), F32)
    for member in range(members):
        mask = own_mask(2 * RANK + 16, member > my_member)
        for group in range(groups):
            position = group * members + member
            fixed = got_ref[position, 4 * RANK :, :].astype(F32)
            maps = jnp.concatenate([fixed[8:16], zero8], axis=0)
            by_s = maps[:, :RANK].astype(BF16)
            by_s = jnp.concatenate(
                [by_s, maps[:, RANK : 2 * RANK].astype(BF16), by_s], axis=1
            )
            by_t = maps[:, 2 * RANK : 3 * RANK] + maps[:, 3 * RANK :]
            here = (my_group == group) & (my_member == member)
            own_s = jnp.where(here, forwards[group], own_s)
            forwards[group], totals[group] = advance(
                forwards[group], totals[group],
                element(got_ref, position) + (by_s, by_t, fixed), mask,
            )
    own_t = jnp.zeros((RANK, WIDE), F32)
    for group in range(groups):
        own_t = jnp.where(my_group == group, totals[group][RANK : 2 * RANK], own_t)
    own = own_ref[...]
    map_high, map_low = halves(own[:, width : width + 2 * RANK])
    maps = jnp.concatenate([map_high, map_low, map_high], axis=1)
    lanes = lax.broadcasted_iota(I32, own.shape, 1)
    own = jnp.where(lanes < width, own, 0.0) + mm(
        maps, tall(jnp.concatenate([own_t, own_s], axis=0))
    )
    eye = unit(0)[:, :RANK]
    forward = jnp.zeros((RANK, width), F32)
    enter_s = forward
    total = jnp.concatenate([unit(TURN), jnp.zeros((16, WIDE), F32)], axis=0)
    none, rest = jnp.zeros((RANK, WIDE), F32), jnp.zeros((RANK, WIDE - width - RANK), F32)
    row = lax.broadcasted_iota(I32, (RANK + 16, RANK), 0)
    for group in range(groups):
        step, whole = forwards[group], totals[group]
        mass = whole[2 * RANK :]
        ahead = jnp.concatenate(
            [
                step[:, in_s : in_s + RANK] - eye,
                whole[:RANK, in_s : in_s + RANK],
                mass[:, in_s : in_s + RANK],
            ],
            axis=0,
        )
        high, low = halves(ahead)
        enter_s = jnp.where(my_group == group, forward, enter_s)
        moved = mm(jnp.concatenate([high, low, high], axis=1), tall(forward))
        forward = forward + moved[:RANK] + step[:, :width]
        middle = jnp.concatenate(
            [
                whole[:RANK, :width] + moved[RANK : 2 * RANK],
                whole[:RANK, in_t : in_t + RANK] - eye,
                rest,
            ],
            axis=1,
        )
        mask = jnp.where((row < RANK) & (group <= my_group), 0.0, 1.0)
        mass = jnp.concatenate(
            [mass[:, :width] + moved[2 * RANK :], mass[:, in_t : in_t + RANK], rest[:16]], axis=1
        )
        total = gain_step(total, mask, middle) + jnp.concatenate([none, mass], axis=0)
    enter_t = total[:RANK, :width]
    mass = total[RANK:, :width]
    mass_ref[...] = mass[0:2] + mass[2:4]
    map_high, map_low = halves(own[:, width : width + 2 * RANK])
    maps = jnp.concatenate([map_high, map_low, map_high], axis=1)
    state = own[:, :width] + mm(maps, tall(jnp.concatenate([enter_t, enter_s], axis=0)))
    high, low = halves(state)
    blank = jnp.zeros((RANK, width), BF16)
    left = jnp.concatenate([high, high[:RANK], blank], axis=0)
    right = jnp.concatenate([low, blank, blank], axis=0)
    fixed = mm(stack_ref[...], jnp.concatenate([left, right], axis=1))
    potential = solved_ref[...] - (fixed[:, :width] + fixed[:, width:])
    potential_ref[...] = potential.astype(BF16)


def outer(place, got, own, solved, stack):
    panels, width = solved.shape
    return pl.pallas_call(
        outer_kernel,
        in_specs=[SMEM] + [VMEM] * 4,
        out_specs=[VMEM] * 2,
        out_shape=[
            jax.ShapeDtypeStruct((panels, width), BF16),
            jax.ShapeDtypeStruct((2, width), F32),
        ],
        compiler_params=PARAMS,
    )(place, got, own, solved, stack)


def body(
    node_modes, node_index, interp, normals, counts, inverse_diag,
    lower_left, lower_right, upper_left, upper_right, ranks, areas,
):
    devices, width = lax.axis_size(AXES), node_modes.shape[2]
    inner_size, outer_size = lax.axis_size("z"), lax.axis_size(("y", "x"))
    depth, group = lax.axis_index("z"), lax.axis_index(("y", "x"))
    place = jnp.stack([depth, group, lax.axis_index("side"), depth % 2]).astype(I32)
    outgoing = interpolate(node_modes, node_index, interp, normals)
    arrived = lax.all_to_all(
        outgoing.reshape(devices, SLOT_ROWS, width), AXES, split_axis=0, concat_axis=0, tiled=True
    ).reshape(devices * SLOT_ROWS, width)
    right, back = lower_right.T, upper_right.T
    stack, mats, target, scaled, area = prepare(
        place, ranks, counts.reshape(1, devices), inverse_diag, lower_left.T, right,
        upper_left.T, back, areas.reshape(1, -1),
    )
    normal, turned = select(arrived, target, inverse_diag.shape[0])
    other = lax.ppermute(turned, "side", [(0, 1), (1, 0)])
    solved, seen = solve(normal, inverse_diag, right, back)
    send = local(place, solved, scaled, area, turned, other, seen, mats, inner_size)
    got = lax.all_to_all(send, "z", split_axis=0, concat_axis=0, tiled=True)
    own, send = inner(place, got, outer_size)
    got = lax.all_to_all(send, ("y", "x"), split_axis=0, concat_axis=0, tiled=True)
    return outer(place, got, own, solved, stack)


def solution(mesh):
    grid = jax.sharding.Mesh(mesh.devices.reshape(2, 4, 4, 8), ("side",) + AXES)
    in_specs = (
        P(None, AXES, "side"),
        P(None, AXES),
        P(None, AXES),
        P(None, AXES),
        P(None, AXES),
        P(AXES, None),
        P(AXES, None),
        P(AXES, None),
        P(AXES, None),
        P(AXES, None),
        P(AXES),
        P(AXES),
    )
    out_specs = (P(AXES, "side"), P(AXES, "side"))
    return jax.shard_map(body, mesh=grid, in_specs=in_specs, out_specs=out_specs, check_vma=False)
```

```python
import functools
import jax
import jax.numpy as jnp
from jax import lax
from jax.experimental import pallas as pl
from jax.experimental.pallas import tpu as pltpu
from jax.sharding import PartitionSpec as P

F32, BF16, I32 = jnp.float32, jnp.bfloat16, jnp.int32
AXES = ("y", "x", "z")
RANK, CAP, SLOT_ROWS, WIDE = 32, 12, 16, 256
PARAMS = pltpu.CompilerParams(vmem_limit_bytes=28 * 1024 * 1024)
WHOLE = pltpu.CompilerParams(vmem_limit_bytes=62 * 1024 * 1024)
VMEM = pl.BlockSpec(memory_space=pltpu.VMEM)
SMEM = pl.BlockSpec(memory_space=pltpu.SMEM)
HBM = pl.BlockSpec(memory_space=pltpu.HBM)
STEPS, TURN, GROUPS = 4, 128, 4
TILE, LANES, ROWS = 32, 256, 192


def mm(a, b):
    return lax.dot_general(a, b, (((1,), (0,)), ((), ())), preferred_element_type=F32)


def mm_t(a, b):
    return lax.dot_general(a, b, (((1,), (1,)), ((), ())), preferred_element_type=F32)


def halves(value):
    high = value.astype(BF16)
    return high, (value - high.astype(F32)).astype(BF16)


def tall(value):
    high, low = halves(value)
    return jnp.concatenate([high, high, low], axis=0)


def interp_kernel(
    modes_hbm, index_hbm, interp_hbm, normals_hbm, out_hbm,
    modes_ref, index_ref, interp_ref, normals_ref, high_ref, low_ref, out_ref, sems, out_sems,
):
    pairs = [
        (index_hbm, index_ref), (interp_hbm, interp_ref), (normals_hbm, normals_ref),
        (modes_hbm, modes_ref),
    ]
    copies = [
        pltpu.make_async_copy(source, target, sems.at[number])
        for number, (source, target) in enumerate(pairs)
    ]
    for copy in copies:
        copy.start()
    for copy in copies[:3]:
        copy.wait()
    slots, nodes = index_ref.shape[1], modes_ref.shape[1]
    width = modes_ref.shape[2]
    chunk = slots // STEPS
    node = lax.broadcasted_iota(I32, (TILE, nodes), 1).astype(F32)
    leaving = []
    for step in range(STEPS):
        lanes = slice(step * chunk, (step + 1) * chunk)
        rows = jnp.concatenate(
            [
                index_ref[:, lanes].astype(F32),
                interp_ref[:, lanes],
                normals_ref[:, lanes],
                jnp.zeros((5, chunk), F32),
            ],
            axis=0,
        )
        columns = rows.T
        if step == 0:
            copies[3].wait()
        for begin in range(0, chunk, TILE):
            part = columns[begin : begin + TILE]
            for lane in range(0, nodes, LANES):
                mix = jnp.zeros((TILE, LANES), F32)
                for corner in range(4):
                    here = part[:, corner : corner + 1] == node[:, lane : lane + LANES]
                    mix = mix + jnp.where(here, part[:, 4 + corner : 5 + corner], 0.0)
                high, low = halves(mix)
                high_ref[step % 2, begin : begin + TILE, lane : lane + LANES] = high
                low_ref[step % 2, begin : begin + TILE, lane : lane + LANES] = low
        table = jnp.concatenate([modes_ref[0], modes_ref[1], modes_ref[2]], axis=1)
        for begin in range(0, chunk, ROWS):
            picked = mm(high_ref[step % 2, begin : begin + ROWS], table) + mm(
                low_ref[step % 2, begin : begin + ROWS], table
            )
            velocity = jnp.zeros((ROWS, width), F32)
            for axis_id in range(3):
                part = picked[:, axis_id * width : (axis_id + 1) * width]
                normal = columns[begin : begin + ROWS, 8 + axis_id : 9 + axis_id]
                velocity = velocity + normal * part
            blocks = velocity.reshape(ROWS // 24, 24, width)
            where = slice((step * chunk + begin) // 24, (step * chunk + begin + ROWS) // 24)
            out_ref[where, 0:16, :] = blocks[:, 0:16, :].astype(BF16)
            out_ref[where, 16:32, :] = blocks[:, 8:24, :].astype(BF16)
        where = pl.ds(step * chunk // 24, chunk // 24)
        leaving.append(
            pltpu.make_async_copy(out_ref.at[where], out_hbm.at[where], out_sems.at[step])
        )
        leaving[-1].start()
    for copy in leaving:
        copy.wait()


def interpolate(node_modes, node_index, interp, normals):
    slots, width = node_index.shape[1], node_modes.shape[2]
    return pl.pallas_call(
        interp_kernel,
        in_specs=[HBM] * 4,
        out_specs=HBM,
        out_shape=jax.ShapeDtypeStruct((slots // 24, 32, width), BF16),
        scratch_shapes=[
            pltpu.VMEM(node_modes.shape, BF16),
            pltpu.VMEM(node_index.shape, I32),
            pltpu.VMEM(interp.shape, F32),
            pltpu.VMEM(normals.shape, F32),
            pltpu.VMEM((2, slots // STEPS, node_modes.shape[1]), BF16),
            pltpu.VMEM((2, slots // STEPS, node_modes.shape[1]), BF16),
            pltpu.VMEM((slots // 24, 32, width), BF16),
            pltpu.SemaphoreType.DMA((4,)),
            pltpu.SemaphoreType.DMA((STEPS,)),
        ],
        compiler_params=WHOLE,
        cost_estimate=pl.CostEstimate(
            flops=2 * slots * 1024 * 384, bytes_accessed=1 << 20, transcendentals=0
        ),
    )(node_modes, node_index, interp, normals)


def prepare_kernel(
    place_ref, rank_ref, count_ref, diag_ref, lower_ref, right_ref, upper_ref, back_ref, area_ref,
    stack_ref, mats_ref, target_ref, scaled_ref, area_out_ref,
):
    panels = diag_ref.shape[0]
    keep = lax.broadcasted_iota(I32, (RANK, panels), 0) < rank_ref[0]
    zero = jnp.zeros((RANK, panels), BF16)
    lower = jnp.where(keep, lower_ref[...], zero)
    upper = jnp.where(keep, upper_ref[...], zero)
    spread = mm_t(diag_ref[...], lower)
    high, low = halves(spread)
    both = jnp.concatenate([right_ref[...], back_ref[...]], axis=0)
    seen = mm(both, jnp.concatenate([high, low], axis=1))
    seen = seen[:, :RANK] + seen[:, RANK:]
    back = mm_t(back_ref[...], upper)
    blank = jnp.zeros((RANK, RANK), F32)
    mats = jnp.concatenate([-seen[:RANK], -back, seen[RANK:], blank], axis=1)
    mats_high, mats_low = halves(mats)
    mats_ref[...] = jnp.concatenate([mats_high, mats_low], axis=0)
    upper_left = upper.astype(F32).T
    stack_ref[...] = jnp.concatenate(
        [high, upper_left.astype(BF16), low, jnp.zeros((panels, RANK), BF16)], axis=1
    )
    area = jnp.broadcast_to(jnp.broadcast_to(area_ref[...], (8, panels)).T[:, 0:1], (panels, 128))
    area_out_ref[...] = area
    gap = jnp.zeros((panels, 3 * RANK), F32)
    minus = -area[:, :RANK]
    scaled_ref[...] = jnp.concatenate(
        [gap, minus * spread, gap, minus * upper_left], axis=1
    ).astype(BF16)
    sources = count_ref.shape[1]
    slots = target_ref.shape[1]
    counts = jnp.broadcast_to(count_ref[...].astype(F32), (16, sources)).astype(BF16)
    source = lax.broadcasted_iota(I32, (sources, slots), 0)
    column = lax.broadcasted_iota(I32, (sources, slots), 1) // SLOT_ROWS
    start = mm(counts, jnp.where(source < column, 1.0, 0.0).astype(BF16))[0:1]
    mine = mm(counts, jnp.where(source == column, 1.0, 0.0).astype(BF16))[0:1]
    slot = lax.broadcasted_iota(I32, (1, slots), 1) % SLOT_ROWS - 4 * place_ref[3]
    slot = slot.astype(F32)
    target_ref[...] = jnp.where((slot >= 0.0) & (slot < mine), start + slot, -1.0)


def prepare(place, rank, count, diag, lower, right, upper, back, area):
    panels, slots = diag.shape[0], count.shape[1] * SLOT_ROWS
    return pl.pallas_call(
        prepare_kernel,
        in_specs=[SMEM, SMEM] + [VMEM] * 7,
        out_specs=[VMEM] * 5,
        out_shape=[
            jax.ShapeDtypeStruct((panels, 4 * RANK), BF16),
            jax.ShapeDtypeStruct((2 * RANK, 4 * RANK), BF16),
            jax.ShapeDtypeStruct((1, slots), F32),
            jax.ShapeDtypeStruct((panels, 8 * RANK), BF16),
            jax.ShapeDtypeStruct((panels, 4 * RANK), F32),
        ],
        compiler_params=PARAMS,
        cost_estimate=pl.CostEstimate(
            flops=4 << 30, bytes_accessed=8 << 20, transcendentals=0
        ),
    )(place, rank, count, diag, lower, right, upper, back, area)


def select_kernel(arrived_ref, target_ref, normal_ref, turned_ref):
    panels, width = normal_ref.shape
    target = target_ref[...]
    sources = target.shape[1] // SLOT_ROWS
    step = 256
    parts = []
    for begin in range(0, panels, step):
        least = max(0, (begin - CAP + 1) // CAP)
        most = min(sources, (begin + step - 1 + CAP * sources - panels) // CAP + 1)
        first = least * SLOT_ROWS // 128 * 128
        last = -(-most * SLOT_ROWS // 128) * 128
        panel = (lax.broadcasted_iota(I32, (step, last - first), 0) + begin).astype(F32)
        pick = jnp.where(panel == target[:, first:last], 1.0, 0.0).astype(BF16)
        parts.append(mm(pick, arrived_ref[first:last, :]).astype(BF16))
    normal = jnp.concatenate(parts, axis=0)
    normal_ref[...] = normal
    row = lax.broadcasted_iota(I32, (width, width), 0)
    mode = (row % 16) // 2 * 16 + row // 16 * 2 + row % 2
    order = jnp.where(lax.broadcasted_iota(I32, (width, width), 1) == mode, 1.0, 0.0)
    turned_ref[...] = mm_t(order.astype(BF16), normal).astype(BF16)


def select(arrived, target, panels):
    width = arrived.shape[1]
    return pl.pallas_call(
        select_kernel,
        in_specs=[VMEM] * 2,
        out_specs=[VMEM] * 2,
        out_shape=[
            jax.ShapeDtypeStruct((panels, width), BF16),
            jax.ShapeDtypeStruct((width, panels), BF16),
        ],
        compiler_params=PARAMS,
        cost_estimate=pl.CostEstimate(
            flops=1 << 29, bytes_accessed=2 << 20, transcendentals=0
        ),
    )(arrived, target)


def solve_kernel(normal_ref, diag_ref, right_ref, back_ref, solved_ref, seen_ref):
    solved = mm(diag_ref[...], normal_ref[...])
    solved_ref[...] = solved
    high, low = halves(solved)
    width = solved.shape[1]
    both = jnp.concatenate([right_ref[...], back_ref[...]], axis=0)
    seen = mm(both, jnp.concatenate([high, low], axis=1))
    seen_ref[...] = (seen[:, :width] + seen[:, width:]).astype(BF16)


def solve(normal, diag, right, back):
    panels, width = normal.shape
    return pl.pallas_call(
        solve_kernel,
        in_specs=[VMEM] * 4,
        out_specs=[VMEM] * 2,
        out_shape=[
            jax.ShapeDtypeStruct((panels, width), F32),
            jax.ShapeDtypeStruct((2 * RANK, width), BF16),
        ],
        compiler_params=PARAMS,
        cost_estimate=pl.CostEstimate(
            flops=1 << 29, bytes_accessed=4 << 20, transcendentals=0
        ),
    )(normal, diag, right, back)


def local_kernel(
    place_ref, solved_ref, scaled_ref, area_ref, turned_ref, other_ref, seen_ref, mats_ref,
    send_ref,
):
    width = solved_ref.shape[1]
    peers = send_ref.shape[0]
    part = width // peers
    weighted = (area_ref[...] * solved_ref[...]).astype(BF16)
    factor = jnp.concatenate([weighted, scaled_ref[...]], axis=1)
    own = mm(turned_ref[...], factor)
    other = mm(other_ref[...], factor)
    even = place_ref[2] == 0
    send_ref[:, 0 : 2 * RANK, :] = jnp.broadcast_to(
        seen_ref[...][None], (peers, 2 * RANK, width)
    )
    mats = mats_ref[...].astype(F32)
    for side in range(2):
        rows = jnp.where(even, other, own) if side else jnp.where(even, own, other)
        begin = 4 * RANK + side * part
        fixed = rows[:, :width].astype(BF16)
        send_ref[:, begin : begin + part, :] = fixed.reshape(peers, part, width)
        for which in range(2):
            begin = which * RANK + side * part
            block = rows[:, (1 + which) * width : (2 + which) * width].reshape(peers, part, width)
            block = (block + mats[begin : begin + part][None]).astype(BF16)
            send_ref[:, 2 * RANK + begin : 2 * RANK + begin + part, :] = block


def local(place, solved, scaled, area, turned, other, seen, mats, peers):
    width = solved.shape[1]
    return pl.pallas_call(
        local_kernel,
        in_specs=[SMEM] + [VMEM] * 7,
        out_specs=VMEM,
        out_shape=jax.ShapeDtypeStruct((peers, 5 * RANK, width), BF16),
        compiler_params=PARAMS,
        cost_estimate=pl.CostEstimate(
            flops=1 << 28, bytes_accessed=2 << 20, transcendentals=0
        ),
    )(place, solved, scaled, area, turned, other, seen, mats)


def element(ref, position):
    high = ref[position, 2 * RANK : 3 * RANK, :]
    low = ref[position, 3 * RANK : 4 * RANK, :]

    def wide(which):
        lanes = slice(which * RANK, (which + 1) * RANK)
        return jnp.concatenate([high[:, lanes], low[:, lanes], high[:, lanes]], axis=1)

    vectors = ref[position, 0 : 2 * RANK, :].astype(F32)
    back = high[:, RANK : 2 * RANK].astype(F32) + low[:, RANK : 2 * RANK].astype(F32)
    return vectors[:RANK], vectors[RANK:], [wide(0), wide(2)], back


def gain_step(total, mask, middle):
    factor = total[:, TURN : TURN + RANK]
    if mask is not None:
        factor = factor * mask
    high, low = halves(factor)
    rows, wide = factor.shape[0], middle.shape[1]
    if rows != 3 * RANK:
        return total + mm(jnp.concatenate([high, low, high], axis=1), tall(middle))
    both = jnp.concatenate(halves(middle), axis=1)
    first = mm(jnp.concatenate([high, low], axis=0), both)
    return total + (first[:rows, :wide] + first[rows:, :wide] + first[:rows, wide:])


def unit(offset):
    row = lax.broadcasted_iota(I32, (RANK, WIDE), 0)
    lane = lax.broadcasted_iota(I32, (RANK, WIDE), 1)
    return jnp.where(lane == row + offset, 1.0, 0.0).astype(F32)


def advance(forward, total, parts, mask):
    shift, gain, ahead, back, by_s, by_t, fixed = parts
    width = fixed.shape[1]
    pad = jnp.zeros((RANK, WIDE - width), F32)
    gap, tail = jnp.zeros((RANK, width), F32), jnp.zeros((RANK, WIDE - width - RANK), F32)
    moved = mm(jnp.concatenate(ahead + [by_s], axis=0), tall(forward))
    later = forward + moved[:RANK] + jnp.concatenate([shift, pad], axis=1)
    middle = (
        jnp.concatenate([gain, pad], axis=1)
        + jnp.concatenate([gap, back, tail], axis=1)
        - moved[RANK : 2 * RANK]
    )
    mass = moved[2 * RANK :] + jnp.concatenate([fixed, by_t, tail[: fixed.shape[0]]], axis=1)
    none = jnp.zeros((2 * RANK, WIDE), F32)
    total = gain_step(total, mask, middle) + jnp.concatenate([none, mass], axis=0)
    return later, total


def own_mask(rows, keep):
    row = lax.broadcasted_iota(I32, (rows, RANK), 0)
    return jnp.where((row >= RANK) & (row < 2 * RANK) & jnp.logical_not(keep), 0.0, 1.0)


def start_total(rows):
    head = [unit(TURN), unit(TURN)]
    return jnp.concatenate(head + [jnp.zeros((rows, WIDE), F32)], axis=0)


def inner_kernel(place_ref, got_ref, own_ref, send_ref):
    width = got_ref.shape[2]
    mine = place_ref[0]
    in_t, in_s = TURN, TURN + RANK
    forward, total = unit(in_s), start_total(RANK)
    own_s = jnp.zeros_like(forward)
    blank = jnp.zeros((RANK, RANK), BF16)
    for position in range(got_ref.shape[0]):
        by_s = got_ref[position, 2 * RANK : 3 * RANK, 3 * RANK : 4 * RANK]
        by_t = got_ref[position, 3 * RANK : 4 * RANK, 3 * RANK : 4 * RANK].astype(F32)
        fixed = got_ref[position, 4 * RANK : 5 * RANK, :].astype(F32)
        by_s = jnp.concatenate([by_s, blank, by_s], axis=1)
        own_s = jnp.where(mine == position, forward, own_s)
        forward, total = advance(
            forward, total, element(got_ref, position) + (by_s, by_t, fixed),
            own_mask(3 * RANK, position > mine),
        )
    own_ref[...] = jnp.concatenate([own_s, total[RANK : 2 * RANK]], axis=0)
    eye = unit(0)[:, :RANK]
    mats = jnp.concatenate(
        [
            forward[:, in_s : in_s + RANK] - eye,
            total[:RANK, in_t : in_t + RANK] - eye,
            -total[:RANK, in_s : in_s + RANK],
            jnp.zeros((RANK, RANK), F32),
        ],
        axis=1,
    )
    high, low = halves(mats)
    message = jnp.concatenate(
        [forward[:, :width].astype(BF16), total[:RANK, :width].astype(BF16), high, low], axis=0
    )
    peers = send_ref.shape[0]
    send_ref[:, 0 : 4 * RANK, :] = jnp.broadcast_to(message[None], (peers, 4 * RANK, width))
    mass = total[2 * RANK :]
    fixed_high, fixed_low = halves(mass[:, :width])
    by_s_high, by_s_low = halves(mass[:, in_s : in_s + RANK])
    by_t_high, by_t_low = halves(mass[:, in_t : in_t + RANK])
    maps = jnp.concatenate([by_s_high, by_s_low, by_t_high, by_t_low], axis=1)
    sources = jnp.concatenate([fixed_high, fixed_low, maps, jnp.zeros_like(maps)], axis=0)
    row = lax.broadcasted_iota(I32, (peers * 16, 4 * RANK), 0)
    column = lax.broadcasted_iota(I32, (peers * 16, 4 * RANK), 1)
    slot = row % 16
    block = jnp.where(slot < 4, slot // 2, jnp.where((slot == 8) | (slot == 9), 2, 3))
    pick = jnp.where(column == block * RANK + row // 16 * 2 + slot % 2, 1.0, 0.0).astype(BF16)
    send_ref[:, 4 * RANK :, :] = mm(pick, sources).astype(BF16).reshape(peers, 16, width)


def inner(place, got, peers):
    return pl.pallas_call(
        inner_kernel,
        in_specs=[SMEM, VMEM],
        out_specs=[VMEM] * 2,
        out_shape=[
            jax.ShapeDtypeStruct((2 * RANK, WIDE), F32),
            jax.ShapeDtypeStruct((peers, 4 * RANK + 16, got.shape[2]), BF16),
        ],
        compiler_params=PARAMS,
    )(place, got)


def outer_kernel(
    place_ref, got_ref, own_ref, solved_ref, stack_ref, potential_ref, mass_ref,
):
    width = got_ref.shape[2]
    groups = GROUPS
    members = got_ref.shape[0] // groups
    my_group, my_member = place_ref[1] // members, place_ref[1] % members
    in_t, in_s = TURN, TURN + RANK
    forwards = [unit(in_s)] * groups
    totals = [start_total(16)] * groups
    own_s = jnp.zeros((RANK, WIDE), F32)
    zero8 = jnp.zeros((8, 4 * RANK), F32)
    for member in range(members):
        mask = own_mask(2 * RANK + 16, member > my_member)
        for group in range(groups):
            position = group * members + member
            fixed = got_ref[position, 4 * RANK :, :].astype(F32)
            maps = jnp.concatenate([fixed[8:16], zero8], axis=0)
            by_s = maps[:, :RANK].astype(BF16)
            by_s = jnp.concatenate(
                [by_s, maps[:, RANK : 2 * RANK].astype(BF16), by_s], axis=1
            )
            by_t = maps[:, 2 * RANK : 3 * RANK] + maps[:, 3 * RANK :]
            here = (my_group == group) & (my_member == member)
            own_s = jnp.where(here, forwards[group], own_s)
            forwards[group], totals[group] = advance(
                forwards[group], totals[group],
                element(got_ref, position) + (by_s, by_t, fixed), mask,
            )
    own_t = jnp.zeros((RANK, WIDE), F32)
    for group in range(groups):
        own_t = jnp.where(my_group == group, totals[group][RANK : 2 * RANK], own_t)
    own = own_ref[...]
    map_high, map_low = halves(own[:, width : width + 2 * RANK])
    maps = jnp.concatenate([map_high, map_low, map_high], axis=1)
    lanes = lax.broadcasted_iota(I32, own.shape, 1)
    own = jnp.where(lanes < width, own, 0.0) + mm(
        maps, tall(jnp.concatenate([own_t, own_s], axis=0))
    )
    eye = unit(0)[:, :RANK]
    forward = jnp.zeros((RANK, width), F32)
    enter_s = forward
    total = jnp.concatenate([unit(TURN), jnp.zeros((16, WIDE), F32)], axis=0)
    none, rest = jnp.zeros((RANK, WIDE), F32), jnp.zeros((RANK, WIDE - width - RANK), F32)
    row = lax.broadcasted_iota(I32, (RANK + 16, RANK), 0)
    for group in range(groups):
        step, whole = forwards[group], totals[group]
        mass = whole[2 * RANK :]
        ahead = jnp.concatenate(
            [
                step[:, in_s : in_s + RANK] - eye,
                whole[:RANK, in_s : in_s + RANK],
                mass[:, in_s : in_s + RANK],
            ],
            axis=0,
        )
        high, low = halves(ahead)
        enter_s = jnp.where(my_group == group, forward, enter_s)
        moved = mm(jnp.concatenate([high, low, high], axis=1), tall(forward))
        forward = forward + moved[:RANK] + step[:, :width]
        middle = jnp.concatenate(
            [
                whole[:RANK, :width] + moved[RANK : 2 * RANK],
                whole[:RANK, in_t : in_t + RANK] - eye,
                rest,
            ],
            axis=1,
        )
        mask = jnp.where((row < RANK) & (group <= my_group), 0.0, 1.0)
        mass = jnp.concatenate(
            [mass[:, :width] + moved[2 * RANK :], mass[:, in_t : in_t + RANK], rest[:16]], axis=1
        )
        total = gain_step(total, mask, middle) + jnp.concatenate([none, mass], axis=0)
    enter_t = total[:RANK, :width]
    mass = total[RANK:, :width]
    mass_ref[...] = mass[0:2] + mass[2:4]
    map_high, map_low = halves(own[:, width : width + 2 * RANK])
    maps = jnp.concatenate([map_high, map_low, map_high], axis=1)
    state = own[:, :width] + mm(maps, tall(jnp.concatenate([enter_t, enter_s], axis=0)))
    high, low = halves(state)
    blank = jnp.zeros((RANK, width), BF16)
    left = jnp.concatenate([high, high[:RANK], blank], axis=0)
    right = jnp.concatenate([low, blank, blank], axis=0)
    fixed = mm(stack_ref[...], jnp.concatenate([left, right], axis=1))
    potential = solved_ref[...] - (fixed[:, :width] + fixed[:, width:])
    potential_ref[...] = potential.astype(BF16)


def outer(place, got, own, solved, stack):
    panels, width = solved.shape
    return pl.pallas_call(
        outer_kernel,
        in_specs=[SMEM] + [VMEM] * 4,
        out_specs=[VMEM] * 2,
        out_shape=[
            jax.ShapeDtypeStruct((panels, width), BF16),
            jax.ShapeDtypeStruct((2, width), F32),
        ],
        compiler_params=PARAMS,
    )(place, got, own, solved, stack)


def body(
    node_modes, node_index, interp, normals, counts, inverse_diag,
    lower_left, lower_right, upper_left, upper_right, ranks, areas,
):
    devices, width = lax.axis_size(AXES), node_modes.shape[2]
    inner_size, outer_size = lax.axis_size("z"), lax.axis_size(("y", "x"))
    depth, group = lax.axis_index("z"), lax.axis_index(("y", "x"))
    place = jnp.stack([depth, group, lax.axis_index("side"), depth % 2]).astype(I32)
    outgoing = interpolate(node_modes, node_index, interp, normals)
    arrived = lax.all_to_all(
        outgoing.reshape(devices, SLOT_ROWS, width), AXES, split_axis=0, concat_axis=0, tiled=True
    ).reshape(devices * SLOT_ROWS, width)
    right, back = lower_right.T, upper_right.T
    stack, mats, target, scaled, area = prepare(
        place, ranks, counts.reshape(1, devices), inverse_diag, lower_left.T, right,
        upper_left.T, back, areas.reshape(1, -1),
    )
    normal, turned = select(arrived, target, inverse_diag.shape[0])
    other = lax.ppermute(turned, "side", [(0, 1), (1, 0)])
    solved, seen = solve(normal, inverse_diag, right, back)
    send = local(place, solved, scaled, area, turned, other, seen, mats, inner_size)
    got = lax.all_to_all(send, "z", split_axis=0, concat_axis=0, tiled=True)
    own, send = inner(place, got, outer_size)
    got = lax.all_to_all(send, ("y", "x"), split_axis=0, concat_axis=0, tiled=True)
    return outer(place, got, own, solved, stack)


def solution(mesh):
    grid = jax.sharding.Mesh(mesh.devices.reshape(2, 4, 4, 8), ("side",) + AXES)
    in_specs = (
        P(None, AXES, "side"),
        P(None, AXES),
        P(None, AXES),
        P(None, AXES),
        P(None, AXES),
        P(AXES, None),
        P(AXES, None),
        P(AXES, None),
        P(AXES, None),
        P(AXES, None),
        P(AXES),
        P(AXES),
    )
    out_specs = (P(AXES, "side"), P(AXES, "side"))
    return jax.shard_map(body, mesh=grid, in_specs=in_specs, out_specs=out_specs, check_vma=False)
```
